32 devices in a mesh: occ: 4 (over z), pan: 8 (over y, x, core).
Axes of the slice: x: 2, y: 2, z: 4, core: 2. Of those that a mesh axis runs over, the one named last changes fastest.
Arguments:
- gamma_ia: bfloat16 [2, 1024, 8704], P(None, 'occ', 'pan'), may hold values from -6 to 6
- coef_virt: bfloat16 [10240, 8704], P(None, 'pan'), may hold values from -0.09375 to 0.09375
- coef_occ: bfloat16 [10240, 1024], P('occ'), may hold values from -0.1875 to 0.1875
- tile_mask: int32 [80, 80], replicated, may hold values from 0 to 1, as said below
- tile_owner: int32 [80, 80], replicated, may hold values from 0 to 7, as said below
Outputs:
- gradient_tiles: bfloat16 [4, 8, 8, 2, 2, 128, 128], P('occ', 'pan')
The draws below stay inside these ranges and needn't reach their ends.
Inputs may be any that keep to these rules, and one draw needn't show every extreme that they name: `tile_mask`: each block of 20 x 10 tiles holds at most 16 ones. `tile_owner`: within each block of 20 x 10 tiles, at most 2 tiles with tile_mask 1 share an owner; in every draw some block gives exactly 2 such tiles to one owner.
All inputs are finite; a program needn't handle non-finite values.
Results may differ from the reference program's by a relative error of at most 0.005.
Values may be sent and summed in bfloat16 or wider, within the bound.
A program may use at most 128 MiB of HBM per device.

```python
import jax
import jax.numpy as jnp
from jax import lax

NOCC = 1024
NVIR = 8704
NAO = 10240
AUX = 2
TILE = 128
SCAP = 2
NT = 80
MT = 20
NTP = 10
OWNERS = 8
N_OCC = 4
N_PAN = 8


def tile_pattern(key):
    base = jax.random.fold_in(key, 913)
    first = jax.random.fold_in(base, 1)
    second = jax.random.fold_in(base, 2)
    third = jax.random.fold_in(base, 3)
    fourth = jax.random.fold_in(base, 4)
    row_index = lax.broadcasted_iota(jnp.int32, (NT, NT), 0)
    col_index = lax.broadcasted_iota(jnp.int32, (NT, NT), 1)
    spacing = jnp.abs(row_index - col_index)
    limit = jnp.maximum(150, 850 - 25 * spacing)
    screened = (jax.random.randint(first, (NT, NT), 0, 1000) < limit) | (row_index < MT) & (col_index < NTP)
    scores = jax.random.randint(second, (NT, NT), 0, 4096) * (NT * NT) + row_index * NT + col_index
    ordered = jnp.where(screened, scores, scores + 4096 * NT * NT)
    row_blocks = NT // MT
    col_blocks = NT // NTP
    blocked = ordered.reshape(row_blocks, MT, col_blocks, NTP).transpose(0, 2, 1, 3).reshape(row_blocks, col_blocks, MT * NTP)
    places = jnp.argsort(jnp.argsort(blocked, axis=-1), axis=-1).astype(jnp.int32)
    places = places.reshape(row_blocks, col_blocks, MT, NTP).transpose(0, 2, 1, 3).reshape(NT, NT)
    kept = screened & (places < OWNERS * SCAP)
    turns = jax.random.randint(third, (row_blocks, col_blocks), 0, OWNERS)
    turns = jnp.repeat(jnp.repeat(turns, MT, axis=0), NTP, axis=1)
    stray = jax.random.randint(fourth, (NT, NT), 0, OWNERS)
    owners_of = jnp.where(kept, (places + turns) % OWNERS, stray).astype(jnp.int32)
    return (kept.astype(jnp.int32), owners_of)


def draw_tile_mask(key, part):
    return tile_pattern(key)[0]


def draw_tile_owner(key, part):
    return tile_pattern(key)[1]


def strengthened(array, stream_key, source, target, parts, factor):
    def block_of(axis_at):
        return (jnp.arange(array.shape[axis_at]) // (array.shape[axis_at] // parts)).reshape((-1,) + (1,) * (array.ndim - 1 - axis_at))

    first = jax.random.permutation(stream_key, parts)[block_of(target)]
    other_side = (block_of(target) + parts // 2) % parts
    return jnp.where((block_of(source) == first) | (block_of(source) == other_side), factor * array, array)


def steps_of(key, dims, shards, smallest, largest):
    loudness = 1.0
    for axis_at, shards_of in shards:
        steps = jax.random.uniform(jax.random.fold_in(jax.random.fold_in(key, 6), axis_at), (shards_of,), jnp.float32, smallest / len(shards), largest / len(shards))
        loudness = loudness * jnp.repeat(jnp.exp(steps), dims[axis_at] // shards_of).reshape((-1,) + (1,) * (len(dims) - 1 - axis_at))
    return loudness


def scatter_about(own_key, extent, spread, reach, split=(), held_as=jnp.bfloat16):
    gain = steps_of(own_key, extent, split, -0.22, 0.18) if split else 1.0
    drawn = jax.random.normal(own_key, extent, jnp.float32) * spread * gain
    return jnp.minimum(jnp.maximum(drawn, -reach), reach).astype(held_as)


def gaussian_with(key, extent, scale, bound, shards, heavy, held_as=jnp.bfloat16):
    result = scale * jax.random.normal(key, extent, jnp.float32)
    if shards:
        result = result * steps_of(key, extent, shards, -0.22, 0.18)
    return jnp.clip(strengthened(result, jax.random.fold_in(key, 3), *heavy), -bound, bound).astype(held_as)


def setup_inputs(seed: int = 0) -> dict:
    arg_keys = jax.random.split(jax.random.key(seed), 6)
    gamma_ia = scatter_about(arg_keys[0], (AUX, NOCC, NVIR), 1.0, 6.0, ((1, 4), (2, 8)))
    coef_virt = gaussian_with(arg_keys[1], (NAO, NVIR), NVIR ** -0.5, 0.09375, ((1, 8),), (1, 0, 8, 2.0))
    coef_occ = scatter_about(arg_keys[2], (NAO, NOCC), NOCC ** -0.5, 0.1875, ((0, 4),))
    tile_mask = draw_tile_mask(jax.random.fold_in(arg_keys[5], 71), 0)
    tile_owner = draw_tile_owner(jax.random.fold_in(arg_keys[5], 71), 0)
    return {"gamma_ia": gamma_ia, "coef_virt": coef_virt, "coef_occ": coef_occ, "tile_mask": tile_mask, "tile_owner": tile_owner}


def route_slots(block_mask, block_owner, owners):
    usable = block_mask.reshape(-1)
    owners_of = block_owner.reshape(-1)
    belongs = ((usable[:, None] == 1) & (owners_of[:, None] == jnp.arange(owners, dtype=jnp.int32)[None, :])).astype(jnp.int32)
    order_rank = jnp.cumsum(belongs, axis=0) - belongs
    matched = belongs[:, :, None] * (order_rank[:, :, None] == jnp.arange(SCAP, dtype=jnp.int32)[None, None, :]).astype(jnp.int32)
    tile_index = jnp.arange(usable.shape[0], dtype=jnp.int32)
    slot_tile = jnp.sum(matched * tile_index[:, None, None], axis=0).astype(jnp.int32)
    filled = jnp.sum(matched, axis=0)
    return slot_tile, filled


def reference(gamma_ia, coef_virt, coef_occ, tile_mask, tile_owner):
    gamma_flat = gamma_ia.reshape(AUX * NOCC, NVIR)
    half_x = lax.dot_general(gamma_flat, coef_virt, (((1,), (1,)), ((), ())), preferred_element_type=jnp.float32)
    half_x = half_x.astype(jnp.bfloat16).reshape(AUX, NOCC, NAO)

    def one_block(block_id):
        row_block = block_id // N_PAN
        col_block = block_id % N_PAN
        row_coef = lax.dynamic_slice(coef_occ, ((row_block * MT * TILE).astype(jnp.int32), jnp.int32(0)), (MT * TILE, NOCC))
        col_half = lax.dynamic_slice(half_x, (jnp.int32(0), jnp.int32(0), (col_block * NTP * TILE).astype(jnp.int32)), (AUX, NOCC, NTP * TILE))
        products = jnp.einsum("ri,pik->prk", row_coef.astype(jnp.float32), col_half.astype(jnp.float32))
        tile_set = products.reshape(AUX, MT, TILE, NTP, TILE).transpose(1, 3, 0, 2, 4).reshape(MT * NTP, AUX, TILE, TILE)
        block_mask = lax.dynamic_slice(tile_mask, ((row_block * MT).astype(jnp.int32), (col_block * NTP).astype(jnp.int32)), (MT, NTP))
        block_owner = lax.dynamic_slice(tile_owner, ((row_block * MT).astype(jnp.int32), (col_block * NTP).astype(jnp.int32)), (MT, NTP))
        slot_tile, filled = route_slots(block_mask, block_owner, N_PAN)
        picked = jnp.take(tile_set, slot_tile.reshape(-1), axis=0).reshape(N_PAN, SCAP, AUX, TILE, TILE)
        return (picked * filled.astype(jnp.float32)[:, :, None, None, None]).astype(jnp.bfloat16)

    every = lax.map(one_block, jnp.arange(N_OCC * N_PAN, dtype=jnp.int32))
    every = every.reshape(N_OCC, N_PAN, N_PAN, SCAP, AUX, TILE, TILE)
    return every.transpose(0, 2, 1, 3, 4, 5, 6)
```

```python
import functools

import jax
import jax.numpy as jnp
from jax import lax
from jax.experimental import pallas as pl
from jax.experimental.pallas import tpu as pltpu
from jax.sharding import PartitionSpec as P

AUX = 2
TILE = 128
SCAP = 2
PIECES = 2
ROW_CODE = 64
KEPT_CODE = 4096
MESH = pl.DeviceIdType.MESH


def block_codes(tile_mask, tile_owner, row_tiles, col_tiles, owners):
    def body(mask_ref, owner_ref, code_ref):
        first = lax.axis_index("occ") * row_tiles
        shape = mask_ref.shape
        row = lax.broadcasted_iota(jnp.int32, shape, 0) - first
        col = lax.broadcasted_iota(jnp.int32, shape, 1)
        inside = (row >= 0) & (row < row_tiles) & (mask_ref[...] == 1)
        place = (row * ROW_CODE + col).astype(jnp.float32)
        owner = owner_ref[...]
        least, most = [], []
        for j in range(owners):
            chosen = inside & (owner == j)
            least.append(jnp.min(jnp.where(chosen, place, float(1 << 20)), axis=0, keepdims=True))
            most.append(jnp.max(jnp.where(chosen, place, -1.0), axis=0, keepdims=True))
        least, most = jnp.concatenate(least), jnp.concatenate(most)
        lane = lax.broadcasted_iota(jnp.int32, least.shape, 1)
        slot = lax.broadcasted_iota(jnp.int32, code_ref.shape, 1)
        code = jnp.zeros(code_ref.shape, jnp.float32)
        for s in range(owners):
            mine = (lane >= s * col_tiles) & (lane < (s + 1) * col_tiles)
            low = jnp.min(jnp.where(mine, least, float(1 << 20)), axis=1, keepdims=True)
            high = jnp.max(jnp.where(mine, most, -1.0), axis=1, keepdims=True)
            shift = float(KEPT_CODE - s * col_tiles)
            code = jnp.where(slot == SCAP * s, jnp.where(high >= 0.0, low + shift, 0.0), code)
            code = jnp.where(slot == SCAP * s + 1, jnp.where(high > low, high + shift, 0.0), code)
        code_ref[...] = code.astype(jnp.int32)

    return pl.pallas_call(
        body,
        out_shape=jax.ShapeDtypeStruct((owners, 128), jnp.int32),
    )(tile_mask, tile_owner)


def by_collectives(gamma_ia, coef_virt, coef_occ, tile_mask, tile_owner):
    panels = lax.axis_size("pan")
    occ_local = gamma_ia.shape[1]
    panel_width = coef_virt.shape[0] // panels
    row_tiles = coef_occ.shape[0] // TILE
    col_tiles = panel_width // TILE
    gamma_flat = gamma_ia.reshape(AUX * occ_local, gamma_ia.shape[2])
    summed = lax.psum_scatter(
        lax.dot_general(
            coef_virt, gamma_flat, (((1,), (1,)), ((), ())), preferred_element_type=jnp.float32
        ),
        "pan",
        scatter_dimension=0,
        tiled=True,
    )
    half_x = summed.astype(jnp.bfloat16).reshape(panel_width, AUX, occ_local)
    whole_x = lax.all_gather(half_x, "occ", axis=2, tiled=True)
    codes = block_codes(tile_mask, tile_owner, row_tiles, col_tiles, panels)
    codes = lax.dynamic_slice(codes, (0, lax.axis_index("pan") * SCAP), (panels, SCAP)).reshape(-1)
    filled = codes // KEPT_CODE
    row = codes % KEPT_CODE // ROW_CODE
    col = codes % ROW_CODE
    bf16 = jnp.bfloat16
    row_pick = (row[:, None] == jnp.arange(row_tiles)[None, :]).astype(bf16)
    col_pick = (col[:, None] == jnp.arange(col_tiles)[None, :]).astype(bf16)
    row_set = jnp.einsum(
        "st,tri->sri", row_pick, coef_occ.reshape(row_tiles, TILE, coef_occ.shape[1])
    )
    col_set = jnp.einsum(
        "st,tkpi->skpi", col_pick, whole_x.reshape(col_tiles, TILE, AUX, whole_x.shape[2])
    )
    picked = jnp.einsum("sri,skpi->sprk", row_set, col_set, preferred_element_type=jnp.float32)
    picked = (
        picked.reshape(panels, SCAP, AUX, TILE, TILE)
        * filled.astype(jnp.float32).reshape(panels, SCAP)[:, :, None, None, None]
    )
    arrived = lax.all_to_all(
        picked.astype(jnp.bfloat16), "pan", split_axis=0, concat_axis=0, tiled=True
    )
    return arrived[None, None]


def kernel(
    n_occ, n_pan, parts,
    code_of, gamma_ref, virt_ref, occ_ref, out_ref,
    gam, gam_1, virt, coef, y_rows, send_c, recv_c, keep_a, keep_b, send_a, recv_a, send_b, recv_b,
    keep_2, send_2a, recv_2a, send_2b, recv_2b, whole, picked, done,
    load_sem, coef_sem, own_sem, done_sem,
    c_out, c_in, a_out, a_in, b_out, b_in, a2_out, a2_in, b2_out, b2_in,
    g_out, g_in, z_out, z_in, t_out, t_in,
):
    o = lax.axis_index("occ")
    s = lax.axis_index("pan")
    core = lax.rem(s, 2)
    x = lax.rem(s // 2, 2)
    y = s // 4
    other_core = s + 1 - 2 * core
    other_x = s + 2 - 4 * x
    other_y = s + 4 - 8 * y
    group = n_pan // 2
    half = gam_1.shape[0]
    depth = gam_1.shape[1]
    quarter = half // 2
    tiles = quarter * 2 // TILE
    pairs = n_pan // 2
    last = n_occ - 1
    bf16, f32 = jnp.bfloat16, jnp.float32

    def load(pan, t):
        first = pl.multiple_of((pan * (parts * tiles) + t) * TILE, TILE)
        return pltpu.make_async_copy(
            virt_ref.at[:, pl.ds(first, TILE)], virt.at[pan, t], load_sem.at[pan, t]
        )

    def load_part(q):
        for g in range(group):
            for t in range(tiles):
                load(2 * g + 1 - core, q * tiles + t).start()
        for g in range(group):
            for t in range(tiles):
                load(2 * g + core, q * tiles + t).start()

    load_part(0)
    fetch = pltpu.make_async_copy(occ_ref, coef, coef_sem)

    barrier = pltpu.get_barrier_semaphore()
    for d in range(1, n_pan):
        pl.semaphore_signal(
            barrier, inc=1, device_id=(o, lax.rem(s + d, n_pan)), device_id_type=MESH
        )
    for d in range(1, n_occ):
        pl.semaphore_signal(
            barrier, inc=1, device_id=(lax.rem(o + d, n_occ), s), device_id_type=MESH
        )
    gam[pl.ds(pl.multiple_of(o * half, half), half), :] = gamma_ref[0].T
    pl.semaphore_wait(barrier, n_pan + n_occ - 2)

    def remote(src, dst, out_sem, in_sem, pan, row=None):
        return pltpu.make_async_remote_copy(
            src_ref=src, dst_ref=dst, send_sem=out_sem, recv_sem=in_sem,
            device_id=(o if row is None else row, pan), device_id_type=MESH,
        )

    def copy_c(q):
        return remote(send_c.at[q], recv_c.at[q], c_out.at[q], c_in.at[q], other_core)

    def copy_a(q):
        return remote(send_a.at[q], recv_a.at[q], a_out.at[q], a_in.at[q], other_x)

    def copy_b(q):
        return remote(send_b.at[q], recv_b.at[q], b_out.at[q], b_in.at[q], other_y)

    def copy_2a(q):
        return remote(send_2a.at[q], recv_2a.at[q], a2_out.at[q], a2_in.at[q], other_y)

    def copy_2b(q):
        return remote(send_2b.at[q], recv_2b.at[q], b2_out.at[q], b2_in.at[q], other_x)

    def beyond(way):
        return jnp.clip(o + 1 - 2 * way, 0, last)

    def copy_g(q, way, hop, source):
        rows = half // PIECES
        first = pl.multiple_of(source * half + q * rows, rows)
        part = gam.at[pl.ds(first, rows)]
        return remote(
            part, part, g_out.at[way, hop, q], g_in.at[way, hop, q], s, beyond(way)
        )

    def copy_z(q, way, hop, source):
        part = whole.at[source, pl.ds(q * tiles, tiles)]
        return remote(
            part, part, z_out.at[way, hop, q], z_in.at[way, hop, q], s, beyond(way)
        )

    def sends(way, hop):
        return (o < last) & (o >= hop) if way == 0 else (o > 0) & (o + hop <= last)

    def held(way, hop):
        return o - hop if way == 0 else o + hop

    def pass_on(copy, count, hop, when=True):
        for way in range(2):
            @pl.when(sends(way, hop) & when)
            def _(way=way):
                def one(q, c):
                    if hop:
                        copy(q, way, hop - 1, held(way, hop)).wait_recv()
                    copy(q, way, hop, held(way, hop)).start()
                    return c

                lax.fori_loop(0, count, one, 0)

    def all_here(copy, count):
        for hop in range(1, n_occ):
            for way, end in ((0, last), (1, 0)):
                @pl.when(o == end)
                def _(hop=hop, way=way):
                    def arrive(q, c):
                        copy(q, way, hop - 1, held(way, hop)).wait_recv()
                        return c

                    lax.fori_loop(0, count, arrive, 0)

    pass_on(copy_g, PIECES, 0)
    gam_1[...] = gamma_ref[1].T

    def product(q, pan):
        columns = jnp.concatenate([virt[pan, q * tiles + t] for t in range(tiles)], axis=1)
        return jnp.dot(gam_1[...], columns, preferred_element_type=f32)

    def second(ch):
        copy_a(ch).wait_recv()
        send_2a[ch] = (keep_a[1] + recv_a[ch, 1].astype(f32)).astype(bf16)
        copy_2a(ch).start()
        copy_b(ch).wait_recv()
        send_2b[ch] = (keep_b[1] + recv_b[ch, 1].astype(f32)).astype(bf16)
        copy_2b(ch).start()
        keep_2[0] = keep_a[0] + recv_a[ch, 0].astype(f32)
        keep_2[1] = keep_b[0] + recv_b[ch, 0].astype(f32)

    def third(ch, store):
        copy_2a(ch).wait_recv()
        copy_2b(ch).wait_recv()
        for h, arrived in ((0, recv_2a), (1, recv_2b)):
            total = keep_2[h] + arrived[ch].astype(f32)
            total = total.astype(bf16)
            for t in range(tiles):
                store(h, t, total[:, t * TILE:(t + 1) * TILE])

    def near(b, a):
        return (y + b - 2 * y * b) * 2 + x + a - 2 * x * a

    def half_step(it, carry):
        @pl.when(it + 1 < parts)
        def _():
            load_part(it + 1)

        @pl.when(it == parts)
        def _():
            fetch.start()

        @pl.when(it >= 3)
        def _():
            q = it - 3

            def store(h, t, tile):
                whole[o, q * tiles + t, h * quarter:(h + 1) * quarter] = tile

            third(q, store)

        @pl.when((it >= 2) & (it < parts + 2))
        def _():
            second(it - 2)

        @pl.when((it >= 1) & (it < parts + 1))
        def _():
            q = it - 1
            for g in range(group):
                for t in range(tiles):
                    load(2 * g + core, q * tiles + t).wait()
            copy_c(q).wait_recv()
            for b, a in ((1, 1), (0, 1), (1, 0), (0, 0)):
                g = near(b, a)
                total = product(q, 2 * g + core) + recv_c[q, g].astype(f32)
                if a:
                    send_a[q, b] = total[:quarter].astype(bf16)
                else:
                    keep_a[b] = total[:quarter]
                if b:
                    send_b[q, a] = total[quarter:].astype(bf16)
                else:
                    keep_b[a] = total[quarter:]
                if (b, a) == (0, 1):
                    copy_a(q).start()
                if (b, a) == (1, 0):
                    copy_b(q).start()

        @pl.when(it < parts)
        def _():
            for g in range(group):
                for t in range(tiles):
                    load(2 * g + 1 - core, it * tiles + t).wait()

            def one(g, c):
                send_c[it, g] = product(it, 2 * g + 1 - core).astype(bf16)
                return c

            lax.fori_loop(0, group, one, 0)
            copy_c(it).start()

        pass_on(copy_g, PIECES, 1, it == 2)
        pass_on(copy_g, PIECES, 2, it == parts)
        return carry

    lax.fori_loop(0, parts + 3, half_step, 0)

    pass_on(copy_z, parts, 0)
    fetch.wait()
    all_here(copy_g, PIECES)

    def rows_step(r, carry):
        left = jnp.concatenate([coef[2 * r], coef[2 * r + 1]])
        for first in range(0, depth, 256):
            end = min(first + 256, depth)
            made = jnp.dot(left, gam[:, first:end], preferred_element_type=f32).astype(bf16)
            y_rows[2 * r, :, first:end] = made[:TILE]
            y_rows[2 * r + 1, :, first:end] = made[TILE:]
        return carry

    lax.fori_loop(0, coef.shape[0] // 2, rows_step, 0)

    def place(panel, j, k):
        code = code_of[j, SCAP * panel + k]
        kept = lax.shift_right_logical(code, 12)
        row = lax.shift_right_logical(code - kept * KEPT_CODE, 6)
        return row, code - kept * KEPT_CODE - row * ROW_CODE, kept.astype(f32)

    def tile_part(panel, j, k):
        row, col, kept = place(panel, j, k)
        return jnp.dot(y_rows[row], virt[panel, col], preferred_element_type=f32) * kept

    def tile_step(it, carry):
        @pl.when(it >= 3)
        def _():
            pair = it - 3

            def store(h, t, tile):
                done[2 * pair + t, h] = tile

            third(parts + pair, store)

        @pl.when((it >= 2) & (it < pairs + 2))
        def _():
            second(parts + it - 2)

        @pl.when((it >= 1) & (it < pairs + 1))
        def _():
            pair = it - 1
            ch = parts + pair
            copy_c(ch).wait_recv()
            for b, a in ((1, 1), (0, 1), (1, 0), (0, 0)):
                g = near(b, a)
                j = 2 * g + core
                for k in range(SCAP):
                    for t in range(2):
                        rows = slice(k * TILE, (k + 1) * TILE)
                        cols = slice(t * TILE, (t + 1) * TILE)
                        total = tile_part(2 * pair + t, j, k)
                        total = total + recv_c[ch, g, rows, cols].astype(f32)
                        if k == 0 and a:
                            send_a[ch, b, :, cols] = total.astype(bf16)
                        elif k == 0:
                            keep_a[b, :, cols] = total
                        elif b:
                            send_b[ch, a, :, cols] = total.astype(bf16)
                        else:
                            keep_b[a, :, cols] = total
                if (b, a) == (0, 1):
                    copy_a(ch).start()
                if (b, a) == (1, 0):
                    copy_b(ch).start()

        @pl.when(it < pairs)
        def _():
            ch = parts + it

            def one(g, c):
                for k in range(SCAP):
                    for t in range(2):
                        made = tile_part(2 * it + t, 2 * g + 1 - core, k)
                        send_c[
                            ch, g, k * TILE:(k + 1) * TILE, t * TILE:(t + 1) * TILE
                        ] = made.astype(bf16)
                return c

            lax.fori_loop(0, group, one, 0)
            copy_c(ch).start()

        pass_on(copy_z, parts, 1, it == 2)
        return carry

    lax.fori_loop(0, pairs + 3, tile_step, 0)

    pass_on(copy_z, parts, 2)
    finished = pltpu.make_async_copy(done, out_ref.at[:, :, 0], done_sem)
    finished.start()

    def tile_send(d, source, target):
        return remote(
            picked.at[target], out_ref.at[source, :, 1], t_out.at[d - 1], t_in.at[d - 1], target
        )

    own = pltpu.make_async_copy(picked.at[s], out_ref.at[s, :, 1], own_sem)

    all_here(copy_z, parts)

    def one_owner(d, c):
        j = lax.rem(s + d, n_pan)
        for k in range(SCAP):
            row, col, kept = place(s, j, k)
            total = jnp.dot(
                coef[row],
                jnp.concatenate([whole[z, col] for z in range(n_occ)]),
                preferred_element_type=f32,
            )
            picked[j, k] = (total * kept).astype(bf16)

        @pl.when(d < n_pan)
        def _():
            tile_send(d, s, j).start()

        return c

    lax.fori_loop(1, n_pan + 1, one_owner, 0)
    own.start()

    def drain(ch, c):
        for copy in (copy_c, copy_a, copy_b, copy_2a, copy_2b):
            copy(ch).wait_send()
        return c

    lax.fori_loop(0, parts + pairs, drain, 0)

    for copy, count in ((copy_g, PIECES), (copy_z, parts)):
        for hop in range(last):
            for way in range(2):
                @pl.when(sends(way, hop))
                def _(copy=copy, count=count, hop=hop, way=way):
                    def drain_z(q, c):
                        copy(q, way, hop, held(way, hop)).wait_send()
                        return c

                    lax.fori_loop(0, count, drain_z, 0)

    def finish(d, c):
        tile_send(d, s, lax.rem(s + d, n_pan)).wait_send()
        source = lax.rem(s + n_pan - d, n_pan)
        tile_send(d, source, source).wait_recv()
        return c

    lax.fori_loop(1, n_pan, finish, 0)
    finished.wait()
    own.wait()


def by_kernel(n_occ, n_pan, gamma_ia, coef_virt, coef_occ, tile_mask, tile_owner):
    half = gamma_ia.shape[1]
    depth = gamma_ia.shape[2]
    panel_width = coef_virt.shape[0] // n_pan
    row_tiles = coef_occ.shape[0] // TILE
    col_tiles = panel_width // TILE
    parts = col_tiles // 2
    width = 2 * TILE
    pairs = n_pan // 2
    chunks = parts + pairs
    group = n_pan // 2
    quarter = half // 2
    codes = block_codes(tile_mask, tile_owner, row_tiles, col_tiles, n_pan)
    bf16, f32 = jnp.bfloat16, jnp.float32
    dma = pltpu.SemaphoreType.DMA
    hbm = pl.BlockSpec(memory_space=pl.ANY)
    arrived = pl.pallas_call(
        functools.partial(kernel, n_occ, n_pan, parts),
        out_shape=jax.ShapeDtypeStruct((n_pan, SCAP, AUX, TILE, TILE), bf16),
        in_specs=[
            pl.BlockSpec(memory_space=pltpu.SMEM), pl.BlockSpec(memory_space=pltpu.VMEM), hbm, hbm
        ],
        out_specs=hbm,
        scratch_shapes=[
            pltpu.VMEM((n_occ * half, depth), bf16),
            pltpu.VMEM((half, depth), bf16),
            pltpu.VMEM((n_pan, col_tiles, depth, TILE), bf16),
            pltpu.VMEM((row_tiles, TILE, coef_occ.shape[1]), bf16),
            pltpu.VMEM((row_tiles, TILE, depth), bf16),
            pltpu.VMEM((chunks, group, half, width), bf16),
            pltpu.VMEM((chunks, group, half, width), bf16),
            pltpu.VMEM((2, quarter, width), f32),
            pltpu.VMEM((2, quarter, width), f32),
            pltpu.VMEM((chunks, 2, quarter, width), bf16),
            pltpu.VMEM((chunks, 2, quarter, width), bf16),
            pltpu.VMEM((chunks, 2, quarter, width), bf16),
            pltpu.VMEM((chunks, 2, quarter, width), bf16),
            pltpu.VMEM((2, quarter, width), f32),
            pltpu.VMEM((chunks, quarter, width), bf16),
            pltpu.VMEM((chunks, quarter, width), bf16),
            pltpu.VMEM((chunks, quarter, width), bf16),
            pltpu.VMEM((chunks, quarter, width), bf16),
            pltpu.VMEM((n_occ, col_tiles, half, TILE), bf16),
            pltpu.VMEM((n_pan, SCAP, TILE, TILE), bf16),
            pltpu.VMEM((n_pan, SCAP, TILE, TILE), bf16),
            dma((n_pan, col_tiles)), dma, dma, dma,
            *[dma((chunks,)) for _ in range(10)],
            dma((2, n_occ - 1, PIECES)), dma((2, n_occ - 1, PIECES)),
            dma((2, n_occ - 1, parts)), dma((2, n_occ - 1, parts)),
            dma((n_pan - 1,)), dma((n_pan - 1,)),
        ],
        compiler_params=pltpu.CompilerParams(
            collective_id=0, has_side_effects=True, vmem_limit_bytes=67043328
        ),
    )(
        codes,
        jnp.swapaxes(gamma_ia, 1, 2),
        coef_virt.T,
        coef_occ.reshape(row_tiles, TILE, coef_occ.shape[1]),
    )
    return arrived[None, None]


def solution(mesh):
    n_occ, n_pan = mesh.shape["occ"], mesh.shape["pan"]

    def local(gamma_ia, coef_virt, coef_occ, tile_mask, tile_owner):
        fits = (
            n_pan == 8
            and gamma_ia.shape[1] == 2 * TILE
            and coef_virt.shape[0] % (2 * TILE * n_pan) == 0
            and coef_occ.shape[0] % (2 * TILE) == 0
        )
        if fits:
            return by_kernel(n_occ, n_pan, gamma_ia, coef_virt, coef_occ, tile_mask, tile_owner)
        return by_collectives(gamma_ia, coef_virt, coef_occ, tile_mask, tile_owner)

    return jax.shard_map(
        local,
        mesh=mesh,
        in_specs=(P(None, "occ", "pan"), P(None, "pan"), P("occ", None), P(), P()),
        out_specs=P("occ", "pan", None, None, None, None, None),
        check_vma=False,
    )
```

```python
import functools

import jax
import jax.numpy as jnp
from jax import lax
from jax.experimental import pallas as pl
from jax.experimental.pallas import tpu as pltpu
from jax.sharding import PartitionSpec as P

AUX = 2
TILE = 128
SCAP = 2
PIECE = 256
LAGS = (1, 3, 5)
ROW_CODE = 64
KEPT_CODE = 4096
MESH = pl.DeviceIdType.MESH


def block_codes(tile_mask, tile_owner, row_tiles, col_tiles, owners, blocks):
    count = len(blocks(0))

    def body(mask_ref, owner_ref, code_ref):
        shape = mask_ref.shape
        col = lax.broadcasted_iota(jnp.int32, shape, 1)
        owner = jnp.where(mask_ref[...] == 1, owner_ref[...], -1)
        for n, block in enumerate(blocks(lax.axis_index("occ"))):
            row = lax.broadcasted_iota(jnp.int32, shape, 0) - block * row_tiles
            inside = (row >= 0) & (row < row_tiles)
            place = (row * ROW_CODE + col).astype(jnp.float32)
            owner_of = jnp.where(inside, owner, -1)
            least, most = [], []
            for j in range(owners):
                chosen = owner_of == j
                least.append(
                    jnp.min(jnp.where(chosen, place, float(1 << 20)), axis=0, keepdims=True)
                )
                most.append(jnp.max(jnp.where(chosen, place, -1.0), axis=0, keepdims=True))
            least, most = jnp.concatenate(least), jnp.concatenate(most)
            lane = lax.broadcasted_iota(jnp.int32, least.shape, 1)
            slot = lax.broadcasted_iota(jnp.int32, (owners, TILE), 1)
            code = jnp.zeros((owners, TILE), jnp.float32)
            for s in range(owners):
                mine = (lane >= s * col_tiles) & (lane < (s + 1) * col_tiles)
                low = jnp.min(jnp.where(mine, least, float(1 << 20)), axis=1, keepdims=True)
                high = jnp.max(jnp.where(mine, most, -1.0), axis=1, keepdims=True)
                shift = float(KEPT_CODE - s * col_tiles)
                one = jnp.where(high >= 0.0, low + shift, 0.0)
                two = jnp.where(high > low, high + shift, 0.0)
                code = jnp.where(slot == SCAP * s, one, code)
                code = jnp.where(slot == SCAP * s + 1, two, code)
            code_ref[n * owners:(n + 1) * owners, :] = code.astype(jnp.int32)

    return pl.pallas_call(
        body,
        out_shape=jax.ShapeDtypeStruct((count * owners, TILE), jnp.int32),
    )(tile_mask, tile_owner)


def by_collectives(gamma_ia, coef_virt, coef_occ, tile_mask, tile_owner):
    panels = lax.axis_size("pan")
    occ_local = gamma_ia.shape[1]
    panel_width = coef_virt.shape[0] // panels
    row_tiles = coef_occ.shape[0] // TILE
    col_tiles = panel_width // TILE
    gamma_flat = gamma_ia.reshape(AUX * occ_local, gamma_ia.shape[2])
    summed = lax.psum_scatter(
        lax.dot_general(
            coef_virt, gamma_flat, (((1,), (1,)), ((), ())), preferred_element_type=jnp.float32
        ),
        "pan",
        scatter_dimension=0,
        tiled=True,
    )
    half_x = summed.astype(jnp.bfloat16).reshape(panel_width, AUX, occ_local)
    whole_x = lax.all_gather(half_x, "occ", axis=2, tiled=True)
    codes = block_codes(
        tile_mask, tile_owner, row_tiles, col_tiles, panels, lambda o: (o,)
    )
    codes = lax.dynamic_slice(codes, (0, lax.axis_index("pan") * SCAP), (panels, SCAP)).reshape(-1)
    filled = codes // KEPT_CODE
    row = codes % KEPT_CODE // ROW_CODE
    col = codes % ROW_CODE
    bf16 = jnp.bfloat16
    row_pick = (row[:, None] == jnp.arange(row_tiles)[None, :]).astype(bf16)
    col_pick = (col[:, None] == jnp.arange(col_tiles)[None, :]).astype(bf16)
    row_set = jnp.einsum(
        "st,tri->sri", row_pick, coef_occ.reshape(row_tiles, TILE, coef_occ.shape[1])
    )
    col_set = jnp.einsum(
        "st,tkpi->skpi", col_pick, whole_x.reshape(col_tiles, TILE, AUX, whole_x.shape[2])
    )
    picked = jnp.einsum("sri,skpi->sprk", row_set, col_set, preferred_element_type=jnp.float32)
    picked = (
        picked.reshape(panels, SCAP, AUX, TILE, TILE)
        * filled.astype(jnp.float32).reshape(panels, SCAP)[:, :, None, None, None]
    )
    arrived = lax.all_to_all(
        picked.astype(jnp.bfloat16), "pan", split_axis=0, concat_axis=0, tiled=True
    )
    return arrived[None, None]


def kernel(
    n_occ, n_pan, parts,
    code_of, gamma_ref, virt_ref, occ_ref, out_ref,
    gam, flat, stage, gam_1, virt, coef, y_rows, send_c, recv_c, keep_a, keep_b,
    send_a, recv_a, send_b, recv_b, send_2a, recv_2a, send_2b, recv_2b,
    whole, picked, done, coef_far, send_f, recv_f,
    load_sem, coef_sem, own_sem, done_sem, gam_sem, stage_sem,
    c_out, c_in, a_out, a_in, b_out, b_in, a2_out, a2_in, b2_out, b2_in,
    g_out, g_in, z_out, z_in, t_out, t_in, e_out, e_in, f_out, f_in,
):
    o = lax.axis_index("occ")
    s = lax.axis_index("pan")
    core = lax.rem(s, 2)
    x = lax.rem(s // 2, 2)
    y = s // 4
    other_core = s + 1 - 2 * core
    other_x = s + 2 - 4 * x
    other_y = s + 4 - 8 * y
    group = n_pan // 2
    half, depth = gam_1.shape
    quarter = half // 2
    tiles = half // TILE
    pairs = n_pan // 2
    last = n_occ - 1
    upper = o // 2
    middle = (o > 0) & (o < last)
    bf16, f32 = jnp.bfloat16, jnp.float32
    pieces = [
        (n * PIECE, PIECE if n + 1 < depth // PIECE else depth - n * PIECE)
        for n in range(depth // PIECE)
    ]

    def load(pan, t):
        first = pl.multiple_of((pan * (parts * tiles) + t) * TILE, TILE)
        return pltpu.make_async_copy(
            virt_ref.at[:, pl.ds(first, TILE)], virt.at[pan, t], load_sem.at[pan, t]
        )

    def load_part(q):
        for g in range(group):
            for t in range(tiles):
                load(2 * g + 1 - core, q * tiles + t).start()
        for g in range(group):
            for t in range(tiles):
                load(2 * g + core, q * tiles + t).start()

    take_0 = pltpu.make_async_copy(gamma_ref.at[0], gam.at[o], gam_sem)
    take_1 = pltpu.make_async_copy(gamma_ref.at[1], stage, stage_sem)
    fetch = pltpu.make_async_copy(occ_ref, coef, coef_sem)
    take_1.start()

    barrier = pltpu.get_barrier_semaphore()
    for d in range(1, n_pan):
        pl.semaphore_signal(
            barrier, inc=1, device_id=(o, lax.rem(s + d, n_pan)), device_id_type=MESH
        )
    for d in range(1, n_occ):
        pl.semaphore_signal(
            barrier, inc=1, device_id=(lax.rem(o + d, n_occ), s), device_id_type=MESH
        )
    load_part(0)
    take_0.start()
    pl.semaphore_wait(barrier, n_pan + n_occ - 2)

    def remote(src, dst, out_sem, in_sem, pan, row=None):
        return pltpu.make_async_remote_copy(
            src_ref=src, dst_ref=dst, send_sem=out_sem, recv_sem=in_sem,
            device_id=(o if row is None else row, pan), device_id_type=MESH,
        )

    def copy_c(n, base):
        ch = base + n
        return remote(send_c.at[n], recv_c.at[ch], c_out.at[ch], c_in.at[ch], other_core)

    def copy_a(n, base):
        ch = base + n
        return remote(send_a.at[n], recv_a.at[ch], a_out.at[ch], a_in.at[ch], other_x)

    def copy_b(n, base):
        ch = base + n
        return remote(send_b.at[n], recv_b.at[ch], b_out.at[ch], b_in.at[ch], other_y)

    def copy_2a(n, base):
        ch = base + n
        return remote(send_2a.at[n], recv_2a.at[ch], a2_out.at[ch], a2_in.at[ch], other_y)

    def copy_2b(n, base):
        ch = base + n
        return remote(send_2b.at[n], recv_2b.at[ch], b2_out.at[ch], b2_in.at[ch], other_x)

    def drain(base, count):
        def one(n, c):
            for copy in (copy_c, copy_a, copy_b, copy_2a, copy_2b):
                copy(n, base).wait_send()
            return c

        lax.fori_loop(0, count, one, 0)

    def beyond(way):
        return jnp.clip(o + 1 - 2 * way, 0, last)

    def held(way, hop):
        return o - hop if way == 0 else o + hop

    def sends(way, hop):
        return (o < last) & (o >= hop) if way == 0 else (o > 0) & (o + hop <= last)

    def passes(way):
        return o == 1 if way == 0 else o == last - 1

    def ends_at(way):
        return o == last if way == 0 else o == 0

    def copy_g(n, way, hop):
        first, size = pieces[n]
        part = gam.at[held(way, hop), pl.ds(first, size)]
        mine = gamma_ref.at[0, pl.ds(first, size)]
        return remote(
            mine if hop == 0 else part, part,
            g_out.at[way, hop, n], g_in.at[way, hop, n], s, beyond(way),
        )

    def got_g(n, way, hop):
        first, size = pieces[n]
        part = gam.at[held(way, hop + 1), pl.ds(first, size)]
        return remote(
            part, part, g_out.at[way, hop, n], g_in.at[way, hop, n], s, beyond(way)
        )

    def pass_g(hop, when=True, some=range(len(pieces))):
        for way in range(2):
            @pl.when(sends(way, hop) & when)
            def _(way=way):
                for n in some:
                    if hop:
                        got_g(n, way, hop - 1).wait_recv()
                    copy_g(n, way, hop).start()

    def flip(z, n):
        first, size = pieces[n]
        rows = pl.ds(pl.multiple_of(z * half, half), half)
        flat[rows, first:first + size] = gam[z, first:first + size].T

    def copy_z(q, way, hop, source):
        part = whole.at[source, pl.ds(q * tiles, tiles)]
        return remote(
            part, part, z_out.at[way, hop, q], z_in.at[way, hop, q], s, beyond(way)
        )

    def each_part(todo):
        def one(q, c):
            todo(q)
            return c

        lax.fori_loop(0, parts, one, 0)

    parity = x + y - 2 * x * y
    some = coef.shape[0] // 4
    cols = 2 * half

    def band(odd):
        return pl.ds((2 * (parity + odd - 2 * parity * odd) + core) * some, some)

    def copy_e0(end):
        first = cols if end == 0 else 0
        return remote(
            occ_ref.at[band(0), :, pl.ds(first, cols)], coef_far.at[band(0)],
            e_out.at[0], e_in.at[0], s, 1 if end == 0 else last - 1,
        )

    def copy_e(step, odd, pan):
        return remote(
            coef_far.at[band(odd)], coef_far.at[band(odd)], e_out.at[step], e_in.at[step], pan
        )

    across = other_x + core * (other_y - other_x)

    pass_g(0)
    for end in (0, last):
        @pl.when(o == end)
        def _(end=end):
            copy_e0(end).start()

    take_1.wait()
    gam_1[...] = stage[...].T

    def second(n, base):
        ch = base + n
        copy_a(n, base).wait_recv()
        send_2a[n] = (keep_a[n, 1] + recv_a[ch, 1].astype(f32)).astype(bf16)
        copy_2a(n, base).start()
        copy_b(n, base).wait_recv()
        send_2b[n] = (keep_b[n, 1] + recv_b[ch, 1].astype(f32)).astype(bf16)
        copy_2b(n, base).start()
        keep_a[n, 0] = keep_a[n, 0] + recv_a[ch, 0].astype(f32)
        keep_b[n, 0] = keep_b[n, 0] + recv_b[ch, 0].astype(f32)

    def third(n, base, store):
        ch = base + n
        copy_2a(n, base).wait_recv()
        copy_2b(n, base).wait_recv()
        for h, keep, arrived in ((0, keep_a, recv_2a), (1, keep_b, recv_2b)):
            total = (keep[n, 0] + arrived[ch].astype(f32)).astype(bf16)
            for t in range(tiles):
                store(h, t, total[:, t * TILE:(t + 1) * TILE])

    def near(b, a):
        return (y + b - 2 * y * b) * 2 + x + a - 2 * x * a

    def product(q, pan):
        columns = jnp.concatenate([virt[pan, q * tiles + t] for t in range(tiles)], axis=1)
        return jnp.dot(gam_1[...], columns, preferred_element_type=f32)

    def half_step(it, carry):
        @pl.when(it + 1 < parts)
        def _():
            load_part(it + 1)

        @pl.when(it == parts)
        def _():
            fetch.start()

        @pl.when(it < parts)
        def _():
            for g in range(group):
                for t in range(tiles):
                    load(2 * g + 1 - core, it * tiles + t).wait()

            def one(g, c):
                send_c[it, g] = product(it, 2 * g + 1 - core).astype(bf16)
                return c

            lax.fori_loop(0, group, one, 0)
            copy_c(it, 0).start()

        @pl.when((it >= LAGS[0]) & (it < parts + LAGS[0]))
        def _():
            q = it - LAGS[0]
            for g in range(group):
                for t in range(tiles):
                    load(2 * g + core, q * tiles + t).wait()
            copy_c(q, 0).wait_recv()
            for b, a in ((1, 1), (0, 1), (1, 0), (0, 0)):
                g = near(b, a)
                total = product(q, 2 * g + core) + recv_c[q, g].astype(f32)
                if a:
                    send_a[q, b] = total[:quarter].astype(bf16)
                else:
                    keep_a[q, b] = total[:quarter]
                if b:
                    send_b[q, a] = total[quarter:].astype(bf16)
                else:
                    keep_b[q, a] = total[quarter:]
                if (b, a) == (0, 1):
                    copy_a(q, 0).start()
                if (b, a) == (1, 0):
                    copy_b(q, 0).start()

        pass_g(1, it == 3, (0, 1))
        pass_g(1, it == 5, range(2, len(pieces)))

        @pl.when((it >= LAGS[1]) & (it < parts + LAGS[1]))
        def _():
            second(it - LAGS[1], 0)

        @pl.when(it >= LAGS[2])
        def _():
            q = it - LAGS[2]

            def store(h, t, tile):
                whole[o, q * tiles + t, h * quarter:(h + 1) * quarter] = tile

            third(q, 0, store)

        @pl.when(it == parts)
        def _():
            take_0.wait()
            for n in range(len(pieces)):
                flip(o, n)

        pass_g(2, it == parts + 2, (0, 1))
        pass_g(2, it == parts + 3, (2,))

        for side in (-1, 1):
            @pl.when(middle & (it == parts + 1))
            def _(side=side):
                for n in range(len(pieces)):
                    flip(o + side, n)

        return carry

    lax.fori_loop(0, parts + LAGS[2], half_step, 0)

    pass_g(2, True, range(3, len(pieces)))

    for way in range(2):
        @pl.when(sends(way, 0))
        def _(way=way):
            each_part(lambda q: copy_z(q, way, 0, o).start())

    @pl.when(middle)
    def _():
        copy_e(0, 0, across).wait_recv()
        copy_e(1, 0, across).start()

    fetch.wait()
    for way in range(2):
        @pl.when(ends_at(way))
        def _(way=way):
            for hop in range(last - 1):
                for n in range(len(pieces)):
                    got_g(n, way, hop).wait_recv()
                    flip(held(way, hop + 1), n)

    far_plane = (1 - upper) * last
    for n, (first, size) in enumerate(pieces):
        for way in range(2):
            @pl.when(ends_at(way))
            def _(way=way, n=n):
                got_g(n, way, last - 1).wait_recv()

        flip(far_plane, n)

        def rows_step(r, carry, first=first, size=size):
            left = jnp.concatenate([coef[2 * r], coef[2 * r + 1]])
            made = jnp.dot(
                left, flat[:, first:first + size], preferred_element_type=f32
            ).astype(bf16)
            y_rows[2 * r, :, first:first + size] = made[:TILE]
            y_rows[2 * r + 1, :, first:first + size] = made[TILE:]
            return carry

        lax.fori_loop(0, coef.shape[0] // 2, rows_step, 0)

    @pl.when(middle)
    def _():
        copy_e(2, 0, other_core).start()
        copy_e(1, 1, across).wait_recv()
        copy_e(3, 1, other_core).start()

    drain(0, parts)

    def place(block, panel, j, k):
        code = code_of[block * n_pan + j, SCAP * panel + k]
        kept = lax.shift_right_logical(code, 12)
        row = lax.shift_right_logical(code - kept * KEPT_CODE, 6)
        return row, code - kept * KEPT_CODE - row * ROW_CODE, kept.astype(f32)

    def tile_part(panel, j, k):
        row, col, kept = place(0, panel, j, k)
        return jnp.dot(y_rows[row], virt[panel, col], preferred_element_type=f32) * kept

    def tile_step(it, carry):
        @pl.when(it < pairs)
        def _():
            def one(g, c):
                for k in range(SCAP):
                    for t in range(2):
                        made = tile_part(2 * it + t, 2 * g + 1 - core, k)
                        send_c[
                            it, g, k * TILE:(k + 1) * TILE, t * TILE:(t + 1) * TILE
                        ] = made.astype(bf16)
                return c

            lax.fori_loop(0, group, one, 0)
            copy_c(it, parts).start()

        @pl.when((it >= LAGS[0]) & (it < pairs + LAGS[0]))
        def _():
            pair = it - LAGS[0]
            ch = parts + pair
            copy_c(pair, parts).wait_recv()
            for b, a in ((1, 1), (0, 1), (1, 0), (0, 0)):
                g = near(b, a)
                j = 2 * g + core
                for k in range(SCAP):
                    for t in range(2):
                        rows = slice(k * TILE, (k + 1) * TILE)
                        cols = slice(t * TILE, (t + 1) * TILE)
                        total = tile_part(2 * pair + t, j, k)
                        total = total + recv_c[ch, g, rows, cols].astype(f32)
                        if k == 0 and a:
                            send_a[pair, b, :, cols] = total.astype(bf16)
                        elif k == 0:
                            keep_a[pair, b, :, cols] = total
                        elif b:
                            send_b[pair, a, :, cols] = total.astype(bf16)
                        else:
                            keep_b[pair, a, :, cols] = total
                if (b, a) == (0, 1):
                    copy_a(pair, parts).start()
                if (b, a) == (1, 0):
                    copy_b(pair, parts).start()

        for way in range(2):
            @pl.when(passes(way) & (it == 2))
            def _(way=way):
                def on(q):
                    copy_z(q, way, 0, held(way, 1)).wait_recv()
                    copy_z(q, way, 1, held(way, 1)).start()

                each_part(on)

        @pl.when((it >= LAGS[1]) & (it < pairs + LAGS[1]))
        def _():
            second(it - LAGS[1], parts)

        @pl.when(it >= LAGS[2])
        def _():
            pair = it - LAGS[2]

            def store(h, t, tile):
                done[2 * pair + t, h] = tile

            third(pair, parts, store)

        return carry

    lax.fori_loop(0, pairs + LAGS[0], tile_step, 0)

    def copy_f(j):
        return remote(send_f.at[j], recv_f.at[j], f_out.at[j], f_in.at[j], s, upper * last)

    @pl.when(middle)
    def _():
        for way in range(2):
            @pl.when(passes(1 - way))
            def _(way=way):
                each_part(lambda q: copy_z(q, way, 0, held(way, 1)).wait_recv())
                each_part(lambda q: copy_z(q, way, 1, held(way, 2)).wait_recv())

        copy_e(2, 0, other_core).wait_recv()
        copy_e(3, 1, other_core).wait_recv()
        far = 2 - 2 * upper

        def far_owner(d, c):
            j = lax.rem(s + d, n_pan)
            for k in range(SCAP):
                row, col, kept = place(1, s, j, k)
                total = jnp.dot(
                    coef_far[row],
                    jnp.concatenate([whole[far + z, col] for z in range(2)]),
                    preferred_element_type=f32,
                )
                send_f[j, k] = (total * kept).astype(bf16)
            copy_f(j).start()
            return c

        lax.fori_loop(1, n_pan + 1, far_owner, 0)

    lax.fori_loop(pairs + LAGS[0], pairs + LAGS[2], tile_step, 0)

    finished = pltpu.make_async_copy(done, out_ref.at[:, :, 0], done_sem)
    finished.start()

    def tile_send(d, source, target):
        return remote(
            picked.at[target], out_ref.at[source, :, 1], t_out.at[d - 1], t_in.at[d - 1], target
        )

    own = pltpu.make_async_copy(picked.at[s], out_ref.at[s, :, 1], own_sem)

    def give(d, j):
        @pl.when(d < n_pan)
        def _():
            tile_send(d, s, j).start()

        @pl.when(d == n_pan)
        def _():
            own.start()

    @pl.when(middle)
    def _():
        def one_owner(d, c):
            j = lax.rem(s + d, n_pan)
            for k in range(SCAP):
                row, col, kept = place(0, s, j, k)
                total = jnp.dot(
                    coef[row],
                    jnp.concatenate([whole[z, col] for z in range(n_occ)]),
                    preferred_element_type=f32,
                )
                picked[j, k] = (total * kept).astype(bf16)
            give(d, j)
            return c

        lax.fori_loop(1, n_pan + 1, one_owner, 0)

    for way, end in ((1, 0), (0, last)):
        @pl.when(o == end)
        def _(way=way, end=end):
            each_part(lambda q: copy_z(q, way, 0, held(way, 1)).wait_recv())
            first = 0 if end == 0 else n_occ - 2

            def one_owner(d, c):
                j = lax.rem(s + d, n_pan)
                totals = []
                for k in range(SCAP):
                    row, col, kept = place(0, s, j, k)
                    total = jnp.dot(
                        coef[row, :, first * half:(first + 2) * half],
                        jnp.concatenate([whole[first + z, col] for z in range(2)]),
                        preferred_element_type=f32,
                    )
                    totals.append(total * kept)
                copy_f(j).wait_recv()
                for k in range(SCAP):
                    picked[j, k] = (totals[k] + recv_f[j, k].astype(f32)).astype(bf16)
                give(d, j)
                return c

            lax.fori_loop(1, n_pan + 1, one_owner, 0)
            copy_e0(end).wait_send()

    @pl.when(middle)
    def _():
        copy_e(1, 0, across).wait_send()
        copy_e(2, 0, other_core).wait_send()
        copy_e(3, 1, other_core).wait_send()

        def sent(j, c):
            copy_f(j).wait_send()
            return c

        lax.fori_loop(0, n_pan, sent, 0)

    drain(parts, pairs)

    for way in range(2):
        for hop in range(last):
            @pl.when(sends(way, hop))
            def _(hop=hop, way=way):
                for n in range(len(pieces)):
                    copy_g(n, way, hop).wait_send()

        @pl.when(sends(way, 0))
        def _(way=way):
            each_part(lambda q: copy_z(q, way, 0, o).wait_send())

        @pl.when(passes(way))
        def _(way=way):
            each_part(lambda q: copy_z(q, way, 1, held(way, 1)).wait_send())

    def finish(d, c):
        tile_send(d, s, lax.rem(s + d, n_pan)).wait_send()
        source = lax.rem(s + n_pan - d, n_pan)
        tile_send(d, source, source).wait_recv()
        return c

    lax.fori_loop(1, n_pan, finish, 0)
    finished.wait()
    own.wait()


def by_kernel(n_occ, n_pan, gamma_ia, coef_virt, coef_occ, tile_mask, tile_owner):
    half = gamma_ia.shape[1]
    depth = gamma_ia.shape[2]
    panel_width = coef_virt.shape[0] // n_pan
    row_tiles = coef_occ.shape[0] // TILE
    col_tiles = panel_width // TILE
    parts = col_tiles // 2
    width = 2 * TILE
    pairs = n_pan // 2
    chunks = parts + pairs
    most = max(parts, pairs)
    group = n_pan // 2
    quarter = half // 2
    far = 2 * half
    codes = block_codes(
        tile_mask, tile_owner, row_tiles, col_tiles, n_pan, lambda o: (o, o // 2 * (n_occ - 1))
    )
    bf16, f32 = jnp.bfloat16, jnp.float32
    dma = pltpu.SemaphoreType.DMA
    hbm = pl.BlockSpec(memory_space=pl.ANY)
    pieces = depth // PIECE
    arrived = pl.pallas_call(
        functools.partial(kernel, n_occ, n_pan, parts),
        out_shape=jax.ShapeDtypeStruct((n_pan, SCAP, AUX, TILE, TILE), bf16),
        in_specs=[pl.BlockSpec(memory_space=pltpu.SMEM), hbm, hbm, hbm],
        out_specs=hbm,
        scratch_shapes=[
            pltpu.VMEM((n_occ, depth, half), bf16),
            pltpu.VMEM((n_occ * half, depth), bf16),
            pltpu.VMEM((depth, half), bf16),
            pltpu.VMEM((half, depth), bf16),
            pltpu.VMEM((n_pan, col_tiles, depth, TILE), bf16),
            pltpu.VMEM((row_tiles, TILE, coef_occ.shape[1]), bf16),
            pltpu.VMEM((row_tiles, TILE, depth), bf16),
            pltpu.VMEM((most, group, half, width), bf16),
            pltpu.VMEM((chunks, group, half, width), bf16),
            pltpu.VMEM((most, 2, quarter, width), f32),
            pltpu.VMEM((most, 2, quarter, width), f32),
            pltpu.VMEM((most, 2, quarter, width), bf16),
            pltpu.VMEM((chunks, 2, quarter, width), bf16),
            pltpu.VMEM((most, 2, quarter, width), bf16),
            pltpu.VMEM((chunks, 2, quarter, width), bf16),
            pltpu.VMEM((most, quarter, width), bf16),
            pltpu.VMEM((chunks, quarter, width), bf16),
            pltpu.VMEM((most, quarter, width), bf16),
            pltpu.VMEM((chunks, quarter, width), bf16),
            pltpu.VMEM((n_occ, col_tiles, half, TILE), bf16),
            pltpu.VMEM((n_pan, SCAP, TILE, TILE), bf16),
            pltpu.VMEM((n_pan, SCAP, TILE, TILE), bf16),
            pltpu.VMEM((row_tiles, TILE, far), bf16),
            pltpu.VMEM((n_pan, SCAP, TILE, TILE), bf16),
            pltpu.VMEM((n_pan, SCAP, TILE, TILE), bf16),
            dma((n_pan, col_tiles)), dma, dma, dma, dma, dma,
            *[dma((chunks,)) for _ in range(10)],
            dma((2, n_occ - 1, pieces)), dma((2, n_occ - 1, pieces)),
            dma((2, 2, parts)), dma((2, 2, parts)),
            dma((n_pan - 1,)), dma((n_pan - 1,)),
            dma((4,)), dma((4,)), dma((n_pan,)), dma((n_pan,)),
        ],
        compiler_params=pltpu.CompilerParams(
            collective_id=0, has_side_effects=True, vmem_limit_bytes=67043328
        ),
    )(
        codes,
        jnp.swapaxes(gamma_ia, 1, 2),
        coef_virt.T,
        coef_occ.reshape(row_tiles, TILE, coef_occ.shape[1]),
    )
    return arrived[None, None]


def solution(mesh):
    n_occ, n_pan = mesh.shape["occ"], mesh.shape["pan"]

    def local(gamma_ia, coef_virt, coef_occ, tile_mask, tile_owner):
        fits = (
            n_occ == 4
            and n_pan == 8
            and gamma_ia.shape[1] == 2 * TILE
            and gamma_ia.shape[2] >= PIECE
            and coef_virt.shape[0] % (2 * TILE * n_pan) == 0
            and coef_occ.shape[0] % (4 * TILE) == 0
        )
        if fits:
            return by_kernel(n_occ, n_pan, gamma_ia, coef_virt, coef_occ, tile_mask, tile_owner)
        return by_collectives(gamma_ia, coef_virt, coef_occ, tile_mask, tile_owner)

    return jax.shard_map(
        local,
        mesh=mesh,
        in_specs=(P(None, "occ", "pan"), P(None, "pan"), P("occ", None), P(), P()),
        out_specs=P("occ", "pan", None, None, None, None, None),
        check_vma=False,
    )
```

```python
import functools

import jax
import jax.numpy as jnp
from jax import lax
from jax.experimental import pallas as pl
from jax.experimental.pallas import tpu as pltpu
from jax.sharding import PartitionSpec as P

AUX = 2
TILE = 128
SCAP = 2
PIECE = 256
LAGS = (1, 3, 5)
ROW_CODE = 64
KEPT_CODE = 4096
MESH = pl.DeviceIdType.MESH


def block_codes(tile_mask, tile_owner, row_tiles, col_tiles, owners, blocks):
    count = len(blocks(0))

    def body(mask_ref, owner_ref, code_ref):
        shape = mask_ref.shape
        col = lax.broadcasted_iota(jnp.int32, shape, 1)
        owner = jnp.where(mask_ref[...] == 1, owner_ref[...], -1)
        for n, block in enumerate(blocks(lax.axis_index("occ"))):
            row = lax.broadcasted_iota(jnp.int32, shape, 0) - block * row_tiles
            inside = (row >= 0) & (row < row_tiles)
            place = (row * ROW_CODE + col).astype(jnp.float32)
            owner_of = jnp.where(inside, owner, -1)
            least, most = [], []
            for j in range(owners):
                chosen = owner_of == j
                least.append(
                    jnp.min(jnp.where(chosen, place, float(1 << 20)), axis=0, keepdims=True)
                )
                most.append(jnp.max(jnp.where(chosen, place, -1.0), axis=0, keepdims=True))
            least, most = jnp.concatenate(least), jnp.concatenate(most)
            lane = lax.broadcasted_iota(jnp.int32, least.shape, 1)
            slot = lax.broadcasted_iota(jnp.int32, (owners, TILE), 1)
            code = jnp.zeros((owners, TILE), jnp.float32)
            for s in range(owners):
                mine = (lane >= s * col_tiles) & (lane < (s + 1) * col_tiles)
                low = jnp.min(jnp.where(mine, least, float(1 << 20)), axis=1, keepdims=True)
                high = jnp.max(jnp.where(mine, most, -1.0), axis=1, keepdims=True)
                shift = float(KEPT_CODE - s * col_tiles)
                one = jnp.where(high >= 0.0, low + shift, 0.0)
                two = jnp.where(high > low, high + shift, 0.0)
                code = jnp.where(slot == SCAP * s, one, code)
                code = jnp.where(slot == SCAP * s + 1, two, code)
            code_ref[n * owners:(n + 1) * owners, :] = code.astype(jnp.int32)

    return pl.pallas_call(
        body,
        out_shape=jax.ShapeDtypeStruct((count * owners, TILE), jnp.int32),
    )(tile_mask, tile_owner)


def by_collectives(gamma_ia, coef_virt, coef_occ, tile_mask, tile_owner):
    panels = lax.axis_size("pan")
    occ_local = gamma_ia.shape[1]
    panel_width = coef_virt.shape[0] // panels
    row_tiles = coef_occ.shape[0] // TILE
    col_tiles = panel_width // TILE
    gamma_flat = gamma_ia.reshape(AUX * occ_local, gamma_ia.shape[2])
    summed = lax.psum_scatter(
        lax.dot_general(
            coef_virt, gamma_flat, (((1,), (1,)), ((), ())), preferred_element_type=jnp.float32
        ),
        "pan",
        scatter_dimension=0,
        tiled=True,
    )
    half_x = summed.astype(jnp.bfloat16).reshape(panel_width, AUX, occ_local)
    whole_x = lax.all_gather(half_x, "occ", axis=2, tiled=True)
    codes = block_codes(
        tile_mask, tile_owner, row_tiles, col_tiles, panels, lambda o: (o,)
    )
    codes = lax.dynamic_slice(codes, (0, lax.axis_index("pan") * SCAP), (panels, SCAP)).reshape(-1)
    filled = codes // KEPT_CODE
    row = codes % KEPT_CODE // ROW_CODE
    col = codes % ROW_CODE
    bf16 = jnp.bfloat16
    row_pick = (row[:, None] == jnp.arange(row_tiles)[None, :]).astype(bf16)
    col_pick = (col[:, None] == jnp.arange(col_tiles)[None, :]).astype(bf16)
    row_set = jnp.einsum(
        "st,tri->sri", row_pick, coef_occ.reshape(row_tiles, TILE, coef_occ.shape[1])
    )
    col_set = jnp.einsum(
        "st,tkpi->skpi", col_pick, whole_x.reshape(col_tiles, TILE, AUX, whole_x.shape[2])
    )
    picked = jnp.einsum("sri,skpi->sprk", row_set, col_set, preferred_element_type=jnp.float32)
    picked = (
        picked.reshape(panels, SCAP, AUX, TILE, TILE)
        * filled.astype(jnp.float32).reshape(panels, SCAP)[:, :, None, None, None]
    )
    arrived = lax.all_to_all(
        picked.astype(jnp.bfloat16), "pan", split_axis=0, concat_axis=0, tiled=True
    )
    return arrived[None, None]


def kernel(
    n_occ, n_pan, parts,
    code_of, gamma_ref, virt_ref, occ_ref, out_ref,
    gam, flat, stage, gam_1, virt, coef, y_rows, send_c, recv_c, keep_a, keep_b,
    send_a, recv_a, send_b, recv_b, send_2a, recv_2a, send_2b, recv_2b,
    whole, picked, done, coef_far, send_f, recv_f,
    load_sem, coef_sem, own_sem, done_sem, gam_sem, stage_sem,
    c_out, c_in, a_out, a_in, b_out, b_in, a2_out, a2_in, b2_out, b2_in,
    g_out, g_in, z_out, z_in, t_out, t_in, e_out, e_in, f_out, f_in,
):
    o = lax.axis_index("occ")
    s = lax.axis_index("pan")
    core = lax.rem(s, 2)
    x = lax.rem(s // 2, 2)
    y = s // 4
    other_core = s + 1 - 2 * core
    other_x = s + 2 - 4 * x
    other_y = s + 4 - 8 * y
    group = n_pan // 2
    half, depth = gam_1.shape
    quarter = half // 2
    tiles = half // TILE
    pairs = n_pan // 2
    last = n_occ - 1
    upper = o // 2
    middle = (o > 0) & (o < last)
    bf16, f32 = jnp.bfloat16, jnp.float32
    pieces = [
        (n * PIECE, PIECE if n + 1 < depth // PIECE else depth - n * PIECE)
        for n in range(depth // PIECE)
    ]

    def load(pan, t):
        first = pl.multiple_of((pan * (parts * tiles) + t) * TILE, TILE)
        return pltpu.make_async_copy(
            virt_ref.at[:, pl.ds(first, TILE)], virt.at[pan, t], load_sem.at[pan, t]
        )

    def load_part(q):
        for g in range(group):
            for t in range(tiles):
                load(2 * g + 1 - core, q * tiles + t).start()
        for g in range(group):
            for t in range(tiles):
                load(2 * g + core, q * tiles + t).start()

    take_0 = pltpu.make_async_copy(gamma_ref.at[0], gam.at[o], gam_sem)
    take_1 = pltpu.make_async_copy(gamma_ref.at[1], stage, stage_sem)
    fetch = pltpu.make_async_copy(occ_ref, coef, coef_sem)
    take_1.start()

    barrier = pltpu.get_barrier_semaphore()
    for d in range(1, n_pan):
        pl.semaphore_signal(
            barrier, inc=1, device_id=(o, lax.rem(s + d, n_pan)), device_id_type=MESH
        )
    for d in range(1, n_occ):
        pl.semaphore_signal(
            barrier, inc=1, device_id=(lax.rem(o + d, n_occ), s), device_id_type=MESH
        )
    load_part(0)
    take_0.start()
    pl.semaphore_wait(barrier, n_pan + n_occ - 2)

    def remote(src, dst, out_sem, in_sem, pan, row=None):
        return pltpu.make_async_remote_copy(
            src_ref=src, dst_ref=dst, send_sem=out_sem, recv_sem=in_sem,
            device_id=(o if row is None else row, pan), device_id_type=MESH,
        )

    def copy_c(n, base):
        ch = base + n
        return remote(send_c.at[n], recv_c.at[ch], c_out.at[ch], c_in.at[ch], other_core)

    def copy_a(n, base):
        ch = base + n
        return remote(send_a.at[n], recv_a.at[ch], a_out.at[ch], a_in.at[ch], other_x)

    def copy_b(n, base):
        ch = base + n
        return remote(send_b.at[n], recv_b.at[ch], b_out.at[ch], b_in.at[ch], other_y)

    def copy_2a(n, base):
        ch = base + n
        return remote(send_2a.at[n], recv_2a.at[ch], a2_out.at[ch], a2_in.at[ch], other_y)

    def copy_2b(n, base):
        ch = base + n
        return remote(send_2b.at[n], recv_2b.at[ch], b2_out.at[ch], b2_in.at[ch], other_x)

    def drain(base, count):
        def one(n, c):
            for copy in (copy_c, copy_a, copy_b, copy_2a, copy_2b):
                copy(n, base).wait_send()
            return c

        lax.fori_loop(0, count, one, 0)

    def beyond(way):
        return jnp.clip(o + 1 - 2 * way, 0, last)

    def held(way, hop):
        return o - hop if way == 0 else o + hop

    def sends(way, hop):
        return (o < last) & (o >= hop) if way == 0 else (o > 0) & (o + hop <= last)

    def passes(way):
        return o == 1 if way == 0 else o == last - 1

    def ends_at(way):
        return o == last if way == 0 else o == 0

    def copy_g(n, way, hop):
        first, size = pieces[n]
        part = gam.at[held(way, hop), pl.ds(first, size)]
        mine = gamma_ref.at[0, pl.ds(first, size)]
        return remote(
            mine if hop == 0 else part, part,
            g_out.at[way, hop, n], g_in.at[way, hop, n], s, beyond(way),
        )

    def got_g(n, way, hop):
        first, size = pieces[n]
        part = gam.at[held(way, hop + 1), pl.ds(first, size)]
        return remote(
            part, part, g_out.at[way, hop, n], g_in.at[way, hop, n], s, beyond(way)
        )

    def pass_g(hop, when=True, some=range(len(pieces))):
        for way in range(2):
            @pl.when(sends(way, hop) & when)
            def _(way=way):
                for n in some:
                    if hop:
                        got_g(n, way, hop - 1).wait_recv()
                    copy_g(n, way, hop).start()

    def flip(z, n):
        first, size = pieces[n]
        rows = pl.ds(pl.multiple_of(z * half, half), half)
        flat[rows, first:first + size] = gam[z, first:first + size].T

    def copy_z(q, way, hop, source):
        part = whole.at[source, pl.ds(q * tiles, tiles)]
        return remote(
            part, part, z_out.at[way, hop, q], z_in.at[way, hop, q], s, beyond(way)
        )

    def each_part(todo):
        def one(q, c):
            todo(q)
            return c

        lax.fori_loop(0, parts, one, 0)

    parity = x + y - 2 * x * y
    some = coef.shape[0] // 4
    cols = 2 * half

    def band(odd):
        return pl.ds((2 * (parity + odd - 2 * parity * odd) + core) * some, some)

    def copy_e0(end):
        first = cols if end == 0 else 0
        return remote(
            occ_ref.at[band(0), :, pl.ds(first, cols)], coef_far.at[band(0)],
            e_out.at[0], e_in.at[0], s, 1 if end == 0 else last - 1,
        )

    def copy_e(step, odd, pan):
        return remote(
            coef_far.at[band(odd)], coef_far.at[band(odd)], e_out.at[step], e_in.at[step], pan
        )

    across = other_x + core * (other_y - other_x)

    pass_g(0)
    for end in (0, last):
        @pl.when(o == end)
        def _(end=end):
            copy_e0(end).start()

    take_1.wait()
    gam_1[...] = stage[...].T

    def second(n, base):
        ch = base + n
        copy_a(n, base).wait_recv()
        send_2a[n] = (keep_a[n, 1] + recv_a[ch, 1].astype(f32)).astype(bf16)
        copy_2a(n, base).start()
        copy_b(n, base).wait_recv()
        send_2b[n] = (keep_b[n, 1] + recv_b[ch, 1].astype(f32)).astype(bf16)
        copy_2b(n, base).start()
        keep_a[n, 0] = keep_a[n, 0] + recv_a[ch, 0].astype(f32)
        keep_b[n, 0] = keep_b[n, 0] + recv_b[ch, 0].astype(f32)

    def third(n, base, store):
        ch = base + n
        copy_2a(n, base).wait_recv()
        copy_2b(n, base).wait_recv()
        for h, keep, arrived in ((0, keep_a, recv_2a), (1, keep_b, recv_2b)):
            total = (keep[n, 0] + arrived[ch].astype(f32)).astype(bf16)
            for t in range(tiles):
                store(h, t, total[:, t * TILE:(t + 1) * TILE])

    def near(b, a):
        return (y + b - 2 * y * b) * 2 + x + a - 2 * x * a

    def product(q, pan):
        columns = jnp.concatenate([virt[pan, q * tiles + t] for t in range(tiles)], axis=1)
        return jnp.dot(gam_1[...], columns, preferred_element_type=f32)

    it_sent = max(parts - 2, 0)

    def half_step(it, carry):
        @pl.when(it + 1 < parts)
        def _():
            load_part(it + 1)

        @pl.when(it == parts)
        def _():
            fetch.start()

        @pl.when(it < parts)
        def _():
            for g in range(group):
                for t in range(tiles):
                    load(2 * g + 1 - core, it * tiles + t).wait()

            def one(g, c):
                send_c[it, g] = product(it, 2 * g + 1 - core).astype(bf16)
                return c

            lax.fori_loop(0, group, one, 0)
            copy_c(it, 0).start()

        @pl.when((it >= LAGS[0]) & (it < parts + LAGS[0]))
        def _():
            q = it - LAGS[0]
            for g in range(group):
                for t in range(tiles):
                    load(2 * g + core, q * tiles + t).wait()
            copy_c(q, 0).wait_recv()
            for b, a in ((1, 1), (0, 1), (1, 0), (0, 0)):
                g = near(b, a)
                total = product(q, 2 * g + core) + recv_c[q, g].astype(f32)
                if a:
                    send_a[q, b] = total[:quarter].astype(bf16)
                else:
                    keep_a[q, b] = total[:quarter]
                if b:
                    send_b[q, a] = total[quarter:].astype(bf16)
                else:
                    keep_b[q, a] = total[quarter:]
                if (b, a) == (0, 1):
                    copy_a(q, 0).start()
                if (b, a) == (1, 0):
                    copy_b(q, 0).start()

        pass_g(1, it == 3, (0, 1))
        pass_g(1, it == 5, range(2, len(pieces)))

        @pl.when((it >= LAGS[1]) & (it < parts + LAGS[1]))
        def _():
            second(it - LAGS[1], 0)

        @pl.when(it >= LAGS[2])
        def _():
            q = it - LAGS[2]

            def store(h, t, tile):
                whole[o, q * tiles + t, h * quarter:(h + 1) * quarter] = tile

            third(q, 0, store)
            for end, way in ((0, 0), (last, 1)):
                @pl.when(o == end)
                def _(way=way):
                    copy_z(q, way, 0, o).start()

        for way in range(2):
            @pl.when(passes(way) & (it == parts + 3))
            def _(way=way):
                for q in range(it_sent):
                    copy_z(q, way, 0, o).start()

        @pl.when(it == parts)
        def _():
            take_0.wait()
            for n in range(len(pieces)):
                flip(o, n)

        pass_g(2, it == parts + 2, (0, 1))
        pass_g(2, it == parts + 3, (2,))

        for side in (-1, 1):
            @pl.when(middle & (it == parts + 1))
            def _(side=side):
                for n in range(len(pieces)):
                    flip(o + side, n)

        return carry

    lax.fori_loop(0, parts + LAGS[2], half_step, 0)

    pass_g(2, True, range(3, len(pieces)))

    for way in range(2):
        @pl.when(passes(way))
        def _(way=way):
            for q in range(it_sent, parts):
                copy_z(q, way, 0, o).start()

    @pl.when(middle)
    def _():
        copy_e(0, 0, across).wait_recv()
        copy_e(1, 0, across).start()

    fetch.wait()
    for way in range(2):
        @pl.when(ends_at(way))
        def _(way=way):
            for hop in range(last - 1):
                for n in range(len(pieces)):
                    got_g(n, way, hop).wait_recv()
                    flip(held(way, hop + 1), n)

    far_plane = (1 - upper) * last
    for span in (range(len(pieces) - 1), range(len(pieces) - 1, len(pieces))):
        for n in span:
            for way in range(2):
                @pl.when(ends_at(way))
                def _(way=way, n=n):
                    got_g(n, way, last - 1).wait_recv()

            flip(far_plane, n)

        def rows_step(r, carry, span=span):
            for pair in (2 * r, 2 * r + 1):
                left = jnp.concatenate([coef[2 * pair], coef[2 * pair + 1]])
                for n in span:
                    first, size = pieces[n]
                    made = jnp.dot(
                        left, flat[:, first:first + size], preferred_element_type=f32
                    ).astype(bf16)
                    y_rows[2 * pair, :, first:first + size] = made[:TILE]
                    y_rows[2 * pair + 1, :, first:first + size] = made[TILE:]
            return carry

        lax.fori_loop(0, coef.shape[0] // 4, rows_step, 0)

    for way in range(2):
        @pl.when(passes(way))
        def _(way=way):
            def on(q):
                copy_z(q, way, 0, held(way, 1)).wait_recv()
                copy_z(q, way, 1, held(way, 1)).start()

            each_part(on)

        @pl.when(passes(1 - way))
        def _(way=way):
            each_part(lambda q: copy_z(q, way, 0, o).start())

    @pl.when(middle)
    def _():
        copy_e(2, 0, other_core).start()
        copy_e(1, 1, across).wait_recv()
        copy_e(3, 1, other_core).start()

    drain(0, parts)

    def place(block, panel, j, k):
        code = code_of[block * n_pan + j, SCAP * panel + k]
        kept = lax.shift_right_logical(code, 12)
        row = lax.shift_right_logical(code - kept * KEPT_CODE, 6)
        return row, code - kept * KEPT_CODE - row * ROW_CODE, kept.astype(f32)

    def tile_part(panel, j, k):
        row, col, kept = place(0, panel, j, k)
        return jnp.dot(y_rows[row], virt[panel, col], preferred_element_type=f32) * kept

    def tile_step(it, carry):
        @pl.when(it < pairs)
        def _():
            def one(g, c):
                for k in range(SCAP):
                    for t in range(2):
                        made = tile_part(2 * it + t, 2 * g + 1 - core, k)
                        send_c[
                            it, g, k * TILE:(k + 1) * TILE, t * TILE:(t + 1) * TILE
                        ] = made.astype(bf16)
                return c

            lax.fori_loop(0, group, one, 0)
            copy_c(it, parts).start()

        @pl.when((it >= LAGS[0]) & (it < pairs + LAGS[0]))
        def _():
            pair = it - LAGS[0]
            ch = parts + pair
            copy_c(pair, parts).wait_recv()
            for b, a in ((1, 1), (0, 1), (1, 0), (0, 0)):
                g = near(b, a)
                j = 2 * g + core
                for k in range(SCAP):
                    for t in range(2):
                        rows = slice(k * TILE, (k + 1) * TILE)
                        cols = slice(t * TILE, (t + 1) * TILE)
                        total = tile_part(2 * pair + t, j, k)
                        total = total + recv_c[ch, g, rows, cols].astype(f32)
                        if k == 0 and a:
                            send_a[pair, b, :, cols] = total.astype(bf16)
                        elif k == 0:
                            keep_a[pair, b, :, cols] = total
                        elif b:
                            send_b[pair, a, :, cols] = total.astype(bf16)
                        else:
                            keep_b[pair, a, :, cols] = total
                if (b, a) == (0, 1):
                    copy_a(pair, parts).start()
                if (b, a) == (1, 0):
                    copy_b(pair, parts).start()

        @pl.when((it >= LAGS[1]) & (it < pairs + LAGS[1]))
        def _():
            second(it - LAGS[1], parts)

        @pl.when(it >= LAGS[2])
        def _():
            pair = it - LAGS[2]

            def store(h, t, tile):
                done[2 * pair + t, h] = tile

            third(pair, parts, store)

        return carry

    lax.fori_loop(0, pairs + LAGS[0], tile_step, 0)

    def copy_f(j):
        return remote(send_f.at[j], recv_f.at[j], f_out.at[j], f_in.at[j], s, upper * last)

    @pl.when(middle)
    def _():
        for way in range(2):
            @pl.when(passes(1 - way))
            def _(way=way):
                each_part(lambda q: copy_z(q, way, 0, held(way, 1)).wait_recv())
                each_part(lambda q: copy_z(q, way, 1, held(way, 2)).wait_recv())

        copy_e(2, 0, other_core).wait_recv()
        copy_e(3, 1, other_core).wait_recv()
        far = 2 - 2 * upper

        def far_owner(d, c):
            j = lax.rem(s + d, n_pan)
            for k in range(SCAP):
                row, col, kept = place(1, s, j, k)
                total = jnp.dot(
                    coef_far[row],
                    jnp.concatenate([whole[far + z, col] for z in range(2)]),
                    preferred_element_type=f32,
                )
                send_f[j, k] = (total * kept).astype(bf16)
            copy_f(j).start()
            return c

        lax.fori_loop(1, n_pan + 1, far_owner, 0)

    lax.fori_loop(pairs + LAGS[0], pairs + LAGS[1], tile_step, 0)
    finished = pltpu.make_async_copy(done, out_ref.at[:, :, 0], done_sem)

    def tile_send(d, source, target):
        return remote(
            picked.at[target], out_ref.at[source, :, 1], t_out.at[d - 1], t_in.at[d - 1], target
        )

    own = pltpu.make_async_copy(picked.at[s], out_ref.at[s, :, 1], own_sem)

    def give(d, j):
        @pl.when(d < n_pan)
        def _():
            tile_send(d, s, j).start()

        @pl.when(d == n_pan)
        def _():
            own.start()

    @pl.when(middle)
    def _():
        def one_owner(d, c):
            j = lax.rem(s + d, n_pan)
            for k in range(SCAP):
                row, col, kept = place(0, s, j, k)
                total = jnp.dot(
                    coef[row],
                    jnp.concatenate([whole[z, col] for z in range(n_occ)]),
                    preferred_element_type=f32,
                )
                picked[j, k] = (total * kept).astype(bf16)
            give(d, j)
            return c

        lax.fori_loop(1, n_pan + 1, one_owner, 0)

    for way, end in ((1, 0), (0, last)):
        @pl.when(o == end)
        def _(way=way, end=end):
            each_part(lambda q: copy_z(q, way, 0, held(way, 1)).wait_recv())
            first = 0 if end == 0 else n_occ - 2

            def one_owner(d, c):
                j = lax.rem(s + d, n_pan)
                totals = []
                for k in range(SCAP):
                    row, col, kept = place(0, s, j, k)
                    total = jnp.dot(
                        coef[row, :, first * half:(first + 2) * half],
                        jnp.concatenate([whole[first + z, col] for z in range(2)]),
                        preferred_element_type=f32,
                    )
                    totals.append(total * kept)
                copy_f(j).wait_recv()
                for k in range(SCAP):
                    picked[j, k] = (totals[k] + recv_f[j, k].astype(f32)).astype(bf16)
                give(d, j)
                return c

            lax.fori_loop(1, n_pan + 1, one_owner, 0)
            copy_e0(end).wait_send()

    lax.fori_loop(pairs + LAGS[1], pairs + LAGS[2], tile_step, 0)
    finished.start()

    @pl.when(middle)
    def _():
        copy_e(1, 0, across).wait_send()
        copy_e(2, 0, other_core).wait_send()
        copy_e(3, 1, other_core).wait_send()

        def sent(j, c):
            copy_f(j).wait_send()
            return c

        lax.fori_loop(0, n_pan, sent, 0)

    drain(parts, pairs)

    for way in range(2):
        for hop in range(last):
            @pl.when(sends(way, hop))
            def _(hop=hop, way=way):
                for n in range(len(pieces)):
                    copy_g(n, way, hop).wait_send()

        @pl.when(sends(way, 0))
        def _(way=way):
            each_part(lambda q: copy_z(q, way, 0, o).wait_send())

        @pl.when(passes(way))
        def _(way=way):
            each_part(lambda q: copy_z(q, way, 1, held(way, 1)).wait_send())

    def finish(d, c):
        tile_send(d, s, lax.rem(s + d, n_pan)).wait_send()
        source = lax.rem(s + n_pan - d, n_pan)
        tile_send(d, source, source).wait_recv()
        return c

    lax.fori_loop(1, n_pan, finish, 0)
    finished.wait()
    own.wait()


def by_kernel(n_occ, n_pan, gamma_ia, coef_virt, coef_occ, tile_mask, tile_owner):
    half = gamma_ia.shape[1]
    depth = gamma_ia.shape[2]
    panel_width = coef_virt.shape[0] // n_pan
    row_tiles = coef_occ.shape[0] // TILE
    col_tiles = panel_width // TILE
    parts = col_tiles // 2
    width = 2 * TILE
    pairs = n_pan // 2
    chunks = parts + pairs
    most = max(parts, pairs)
    group = n_pan // 2
    quarter = half // 2
    far = 2 * half
    codes = block_codes(
        tile_mask, tile_owner, row_tiles, col_tiles, n_pan, lambda o: (o, o // 2 * (n_occ - 1))
    )
    bf16, f32 = jnp.bfloat16, jnp.float32
    dma = pltpu.SemaphoreType.DMA
    hbm = pl.BlockSpec(memory_space=pl.ANY)
    pieces = depth // PIECE
    arrived = pl.pallas_call(
        functools.partial(kernel, n_occ, n_pan, parts),
        out_shape=pltpu.VMEM((n_pan, SCAP, AUX, TILE, TILE), bf16),
        in_specs=[pl.BlockSpec(memory_space=pltpu.SMEM), hbm, hbm, hbm],
        out_specs=hbm,
        scratch_shapes=[
            pltpu.VMEM((n_occ, depth, half), bf16),
            pltpu.VMEM((n_occ * half, depth), bf16),
            pltpu.VMEM((depth, half), bf16),
            pltpu.VMEM((half, depth), bf16),
            pltpu.VMEM((n_pan, col_tiles, depth, TILE), bf16),
            pltpu.VMEM((row_tiles, TILE, coef_occ.shape[1]), bf16),
            pltpu.VMEM((row_tiles, TILE, depth), bf16),
            pltpu.VMEM((most, group, half, width), bf16),
            pltpu.VMEM((chunks, group, half, width), bf16),
            pltpu.VMEM((most, 2, quarter, width), f32),
            pltpu.VMEM((most, 2, quarter, width), f32),
            pltpu.VMEM((most, 2, quarter, width), bf16),
            pltpu.VMEM((chunks, 2, quarter, width), bf16),
            pltpu.VMEM((most, 2, quarter, width), bf16),
            pltpu.VMEM((chunks, 2, quarter, width), bf16),
            pltpu.VMEM((most, quarter, width), bf16),
            pltpu.VMEM((chunks, quarter, width), bf16),
            pltpu.VMEM((most, quarter, width), bf16),
            pltpu.VMEM((chunks, quarter, width), bf16),
            pltpu.VMEM((n_occ, col_tiles, half, TILE), bf16),
            pltpu.VMEM((n_pan, SCAP, TILE, TILE), bf16),
            pltpu.VMEM((n_pan, SCAP, TILE, TILE), bf16),
            pltpu.VMEM((row_tiles, TILE, far), bf16),
            pltpu.VMEM((n_pan, SCAP, TILE, TILE), bf16),
            pltpu.VMEM((n_pan, SCAP, TILE, TILE), bf16),
            dma((n_pan, col_tiles)), dma, dma, dma, dma, dma,
            *[dma((chunks,)) for _ in range(10)],
            dma((2, n_occ - 1, pieces)), dma((2, n_occ - 1, pieces)),
            dma((2, 2, parts)), dma((2, 2, parts)),
            dma((n_pan - 1,)), dma((n_pan - 1,)),
            dma((4,)), dma((4,)), dma((n_pan,)), dma((n_pan,)),
        ],
        compiler_params=pltpu.CompilerParams(
            collective_id=0, has_side_effects=True, vmem_limit_bytes=65000000
        ),
    )(
        codes,
        jnp.swapaxes(gamma_ia, 1, 2),
        coef_virt.T,
        coef_occ.reshape(row_tiles, TILE, coef_occ.shape[1]),
    )
    return arrived[None, None]


def solution(mesh):
    n_occ, n_pan = mesh.shape["occ"], mesh.shape["pan"]

    def local(gamma_ia, coef_virt, coef_occ, tile_mask, tile_owner):
        fits = (
            n_occ == 4
            and n_pan == 8
            and gamma_ia.shape[1] == 2 * TILE
            and gamma_ia.shape[2] >= PIECE
            and coef_virt.shape[0] % (2 * TILE * n_pan) == 0
            and coef_occ.shape[0] % (4 * TILE) == 0
        )
        if fits:
            return by_kernel(n_occ, n_pan, gamma_ia, coef_virt, coef_occ, tile_mask, tile_owner)
        return by_collectives(gamma_ia, coef_virt, coef_occ, tile_mask, tile_owner)

    return jax.shard_map(
        local,
        mesh=mesh,
        in_specs=(P(None, "occ", "pan"), P(None, "pan"), P("occ", None), P(), P()),
        out_specs=P("occ", "pan", None, None, None, None, None),
        check_vma=False,
    )
```

```python
import functools

import jax
import jax.numpy as jnp
from jax import lax
from jax.experimental import pallas as pl
from jax.experimental.pallas import tpu as pltpu
from jax.sharding import PartitionSpec as P

AUX = 2
TILE = 128
SCAP = 2
PIECE = 256
LAGS = (1, 3, 5)
ROW_CODE = 64
KEPT_CODE = 4096
MESH = pl.DeviceIdType.MESH


def find_codes(blocks, mask, owner_in, row_tiles, col_tiles, owners):
    col = lax.broadcasted_iota(jnp.int32, mask.shape, 1)
    owner = jnp.where(mask == 1, owner_in, -1)
    codes = []
    for block in blocks:
        row = lax.broadcasted_iota(jnp.int32, mask.shape, 0) - block * row_tiles
        owner_of = jnp.where((row >= 0) & (row < row_tiles), owner, -1)
        place = row * ROW_CODE + col
        least, most = [], []
        for j in range(owners):
            chosen = owner_of == j
            least.append(jnp.min(jnp.where(chosen, place, 1 << 20), axis=0, keepdims=True))
            most.append(jnp.max(jnp.where(chosen, place, -1), axis=0, keepdims=True))
        least, most = jnp.concatenate(least), jnp.concatenate(most)
        lane = lax.broadcasted_iota(jnp.int32, least.shape, 1)
        slot = lax.broadcasted_iota(jnp.int32, (owners, TILE), 1)
        code = jnp.zeros((owners, TILE), jnp.int32)
        for s in range(owners):
            mine = (lane >= s * col_tiles) & (lane < (s + 1) * col_tiles)
            low = jnp.min(jnp.where(mine, least, 1 << 20), axis=1, keepdims=True)
            high = jnp.max(jnp.where(mine, most, -1), axis=1, keepdims=True)
            shift = KEPT_CODE - s * col_tiles
            code = jnp.where(slot == SCAP * s, jnp.where(high >= 0, low + shift, 0), code)
            code = jnp.where(slot == SCAP * s + 1, jnp.where(high > low, high + shift, 0), code)
        codes.append(code)
    return jnp.concatenate(codes)


def by_collectives(gamma_ia, coef_virt, coef_occ, tile_mask, tile_owner):
    panels = lax.axis_size("pan")
    occ_local = gamma_ia.shape[1]
    panel_width = coef_virt.shape[0] // panels
    row_tiles = coef_occ.shape[0] // TILE
    col_tiles = panel_width // TILE
    gamma_flat = gamma_ia.reshape(AUX * occ_local, gamma_ia.shape[2])
    summed = lax.psum_scatter(
        lax.dot_general(
            coef_virt, gamma_flat, (((1,), (1,)), ((), ())), preferred_element_type=jnp.float32
        ),
        "pan",
        scatter_dimension=0,
        tiled=True,
    )
    half_x = summed.astype(jnp.bfloat16).reshape(panel_width, AUX, occ_local)
    whole_x = lax.all_gather(half_x, "occ", axis=2, tiled=True)
    codes = find_codes(
        [lax.axis_index("occ")], tile_mask, tile_owner, row_tiles, col_tiles, panels
    )
    codes = lax.dynamic_slice(codes, (0, lax.axis_index("pan") * SCAP), (panels, SCAP)).reshape(-1)
    filled = codes // KEPT_CODE
    row = codes % KEPT_CODE // ROW_CODE
    col = codes % ROW_CODE
    bf16 = jnp.bfloat16
    row_pick = (row[:, None] == jnp.arange(row_tiles)[None, :]).astype(bf16)
    col_pick = (col[:, None] == jnp.arange(col_tiles)[None, :]).astype(bf16)
    row_set = jnp.einsum(
        "st,tri->sri", row_pick, coef_occ.reshape(row_tiles, TILE, coef_occ.shape[1])
    )
    col_set = jnp.einsum(
        "st,tkpi->skpi", col_pick, whole_x.reshape(col_tiles, TILE, AUX, whole_x.shape[2])
    )
    picked = jnp.einsum("sri,skpi->sprk", row_set, col_set, preferred_element_type=jnp.float32)
    picked = (
        picked.reshape(panels, SCAP, AUX, TILE, TILE)
        * filled.astype(jnp.float32).reshape(panels, SCAP)[:, :, None, None, None]
    )
    arrived = lax.all_to_all(
        picked.astype(jnp.bfloat16), "pan", split_axis=0, concat_axis=0, tiled=True
    )
    return arrived[None, None]


def pieces_of(depth):
    later = depth // PIECE - 1
    first = (depth - later * PIECE + TILE) // TILE * TILE
    starts = [0] + [first + n * PIECE for n in range(later)] + [depth]
    return [(a, b - a) for a, b in zip(starts[:-1], starts[1:])]


def kernel(
    n_occ, n_pan, parts,
    mask_ref, owner_ref, gamma_ref, virt_ref, occ_ref, out_ref,
    gam, flat, stage, gam_1, virt, coef, y_rows, send_c, recv_c, keep_a, keep_b,
    send_a, recv_a, send_b, recv_b, send_2a, recv_2a, send_2b, recv_2b,
    whole, picked, done, coef_far, send_f, recv_f, near_f, code_in, code_of, code_sem,
    load_sem, coef_sem, own_sem, done_sem, gam_sem, stage_sem,
    c_out, c_in, a_out, a_in, b_out, b_in, a2_out, a2_in, b2_out, b2_in,
    g_out, g_in, z_out, z_in, t_out, t_in, e_out, e_in, f_out, f_in,
):
    o = lax.axis_index("occ")
    s = lax.axis_index("pan")
    core = lax.rem(s, 2)
    x = lax.rem(s // 2, 2)
    y = s // 4
    other_core = s + 1 - 2 * core
    other_x = s + 2 - 4 * x
    other_y = s + 4 - 8 * y
    group = n_pan // 2
    half, depth = gam_1.shape
    quarter = half // 2
    tiles = half // TILE
    pairs = n_pan // 2
    last = n_occ - 1
    upper = o // 2
    middle = (o > 0) & (o < last)
    bf16, f32 = jnp.bfloat16, jnp.float32
    pieces = pieces_of(depth)

    def load(pan, t):
        first = pl.multiple_of((pan * (parts * tiles) + t) * TILE, TILE)
        return pltpu.make_async_copy(
            virt_ref.at[:, pl.ds(first, TILE)], virt.at[pan, t], load_sem.at[pan, t]
        )

    def load_part(q):
        for g in range(group):
            for t in range(tiles):
                load(2 * g + 1 - core, q * tiles + t).start()
        for g in range(group):
            for t in range(tiles):
                load(2 * g + core, q * tiles + t).start()

    take_0 = pltpu.make_async_copy(gamma_ref.at[0], gam.at[o], gam_sem)
    take_1 = pltpu.make_async_copy(gamma_ref.at[1], stage, stage_sem)
    fetch = pltpu.make_async_copy(occ_ref, coef, coef_sem)
    tell = pltpu.make_async_copy(code_in, code_of, code_sem)
    take_1.start()

    barrier = pltpu.get_barrier_semaphore()
    for d in range(1, n_pan):
        pl.semaphore_signal(
            barrier, inc=1, device_id=(o, lax.rem(s + d, n_pan)), device_id_type=MESH
        )
    for d in range(1, n_occ):
        pl.semaphore_signal(
            barrier, inc=1, device_id=(lax.rem(o + d, n_occ), s), device_id_type=MESH
        )
    load_part(0)
    take_0.start()
    pl.semaphore_wait(barrier, n_pan + n_occ - 2)

    def remote(src, dst, out_sem, in_sem, pan, row=None):
        return pltpu.make_async_remote_copy(
            src_ref=src, dst_ref=dst, send_sem=out_sem, recv_sem=in_sem,
            device_id=(o if row is None else row, pan), device_id_type=MESH,
        )

    def copy_c(n, base):
        ch = base + n
        return remote(send_c.at[n], recv_c.at[ch], c_out.at[ch], c_in.at[ch], other_core)

    def copy_a(n, base):
        ch = base + n
        return remote(send_a.at[n], recv_a.at[ch], a_out.at[ch], a_in.at[ch], other_x)

    def copy_b(n, base):
        ch = base + n
        return remote(send_b.at[n], recv_b.at[ch], b_out.at[ch], b_in.at[ch], other_y)

    def copy_2a(n, base):
        ch = base + n
        return remote(send_2a.at[n], recv_2a.at[ch], a2_out.at[ch], a2_in.at[ch], other_y)

    def copy_2b(n, base):
        ch = base + n
        return remote(send_2b.at[n], recv_2b.at[ch], b2_out.at[ch], b2_in.at[ch], other_x)

    def drain(base, count):
        def one(n, c):
            for copy in (copy_c, copy_a, copy_b, copy_2a, copy_2b):
                copy(n, base).wait_send()
            return c

        lax.fori_loop(0, count, one, 0)

    def beyond(way):
        return jnp.clip(o + 1 - 2 * way, 0, last)

    def held(way, hop):
        return o - hop if way == 0 else o + hop

    def sends(way, hop):
        return (o < last) & (o >= hop) if way == 0 else (o > 0) & (o + hop <= last)

    def passes(way):
        return o == 1 if way == 0 else o == last - 1

    def ends_at(way):
        return o == last if way == 0 else o == 0

    def copy_g(n, way, hop):
        first, size = pieces[n]
        part = gam.at[held(way, hop), pl.ds(first, size)]
        mine = gamma_ref.at[0, pl.ds(first, size)]
        return remote(
            mine if hop == 0 else part, part,
            g_out.at[way, hop, n], g_in.at[way, hop, n], s, beyond(way),
        )

    def got_g(n, way, hop):
        first, size = pieces[n]
        part = gam.at[held(way, hop + 1), pl.ds(first, size)]
        return remote(
            part, part, g_out.at[way, hop, n], g_in.at[way, hop, n], s, beyond(way)
        )

    def pass_g(hop, when=True, some=range(len(pieces))):
        for way in range(2):
            @pl.when(sends(way, hop) & when)
            def _(way=way):
                for n in some:
                    if hop:
                        got_g(n, way, hop - 1).wait_recv()
                    copy_g(n, way, hop).start()

    def flip(z, n):
        first, size = pieces[n]
        rows = pl.ds(pl.multiple_of(z * half, half), half)
        flat[rows, first:first + size] = gam[z, first:first + size].T

    def copy_z(q, way, hop, source):
        part = whole.at[source, pl.ds(q * tiles, tiles)]
        return remote(
            part, part, z_out.at[way, hop, q], z_in.at[way, hop, q], s, beyond(way)
        )

    def each_part(todo):
        def one(q, c):
            todo(q)
            return c

        lax.fori_loop(0, parts, one, 0)

    parity = x + y - 2 * x * y
    some = coef.shape[0] // 4
    cols = 2 * half

    def band(odd):
        return pl.ds((2 * (parity + odd - 2 * parity * odd) + core) * some, some)

    def copy_e0(end):
        first = cols if end == 0 else 0
        return remote(
            occ_ref.at[band(0), :, pl.ds(first, cols)], coef_far.at[band(0)],
            e_out.at[0], e_in.at[0], s, 1 if end == 0 else last - 1,
        )

    def copy_e(step, odd, pan):
        return remote(
            coef_far.at[band(odd)], coef_far.at[band(odd)], e_out.at[step], e_in.at[step], pan
        )

    across = other_x + core * (other_y - other_x)

    pass_g(0)
    for end in (0, last):
        @pl.when(o == end)
        def _(end=end):
            copy_e0(end).start()

    take_1.wait()
    gam_1[...] = stage[...].T

    def second(n, base):
        ch = base + n
        copy_a(n, base).wait_recv()
        send_2a[n] = (keep_a[n, 1] + recv_a[ch, 1].astype(f32)).astype(bf16)
        copy_2a(n, base).start()
        copy_b(n, base).wait_recv()
        send_2b[n] = (keep_b[n, 1] + recv_b[ch, 1].astype(f32)).astype(bf16)
        copy_2b(n, base).start()
        keep_a[n, 0] = keep_a[n, 0] + recv_a[ch, 0].astype(f32)
        keep_b[n, 0] = keep_b[n, 0] + recv_b[ch, 0].astype(f32)

    def third(n, base, store):
        ch = base + n
        copy_2a(n, base).wait_recv()
        copy_2b(n, base).wait_recv()
        for h, keep, arrived in ((0, keep_a, recv_2a), (1, keep_b, recv_2b)):
            total = (keep[n, 0] + arrived[ch].astype(f32)).astype(bf16)
            for t in range(tiles):
                store(h, t, total[:, t * TILE:(t + 1) * TILE])

    def near(b, a):
        return (y + b - 2 * y * b) * 2 + x + a - 2 * x * a

    def product(q, pan):
        columns = jnp.concatenate([virt[pan, q * tiles + t] for t in range(tiles)], axis=1)
        return jnp.dot(gam_1[...], columns, preferred_element_type=f32)

    it_sent = max(parts - 2, 0)

    def half_step(it, carry):
        @pl.when(it + 1 < parts)
        def _():
            load_part(it + 1)

        @pl.when(it == parts)
        def _():
            fetch.start()

        @pl.when(it < parts)
        def _():
            for g in range(group):
                for t in range(tiles):
                    load(2 * g + 1 - core, it * tiles + t).wait()

            def one(g, c):
                send_c[it, g] = product(it, 2 * g + 1 - core).astype(bf16)
                return c

            lax.fori_loop(0, group, one, 0)
            copy_c(it, 0).start()

        @pl.when((it >= LAGS[0]) & (it < parts + LAGS[0]))
        def _():
            q = it - LAGS[0]
            for g in range(group):
                for t in range(tiles):
                    load(2 * g + core, q * tiles + t).wait()
            copy_c(q, 0).wait_recv()
            for b, a in ((1, 1), (0, 1), (1, 0), (0, 0)):
                g = near(b, a)
                total = product(q, 2 * g + core) + recv_c[q, g].astype(f32)
                if a:
                    send_a[q, b] = total[:quarter].astype(bf16)
                else:
                    keep_a[q, b] = total[:quarter]
                if b:
                    send_b[q, a] = total[quarter:].astype(bf16)
                else:
                    keep_b[q, a] = total[quarter:]
                if (b, a) == (0, 1):
                    copy_a(q, 0).start()
                if (b, a) == (1, 0):
                    copy_b(q, 0).start()

        pass_g(1, it == 3, (0, 1))
        pass_g(1, it == 5, range(2, len(pieces)))

        @pl.when((it >= LAGS[1]) & (it < parts + LAGS[1]))
        def _():
            second(it - LAGS[1], 0)

        @pl.when(it >= LAGS[2])
        def _():
            q = it - LAGS[2]

            def store(h, t, tile):
                whole[o, q * tiles + t, h * quarter:(h + 1) * quarter] = tile

            third(q, 0, store)
            for end, way in ((0, 0), (last, 1)):
                @pl.when(o == end)
                def _(way=way):
                    copy_z(q, way, 0, o).start()

        for way in range(2):
            @pl.when(passes(way) & (it == parts + 3))
            def _(way=way):
                for q in range(it_sent):
                    copy_z(q, way, 0, o).start()

        @pl.when(it == parts)
        def _():
            code_in[...] = find_codes(
                [o, upper * last], mask_ref[...], owner_ref[...],
                coef.shape[0], parts * tiles, n_pan,
            )
            tell.start()
            take_0.wait()
            for n in range(len(pieces)):
                flip(o, n)

        pass_g(2, it == parts + 2, (0, 1))
        pass_g(2, it == parts + 3, (2,))

        for side in (-1, 1):
            @pl.when(middle & (it == parts + 1))
            def _(side=side):
                for n in range(len(pieces)):
                    flip(o + side, n)

        return carry

    lax.fori_loop(0, parts + LAGS[2], half_step, 0)

    pass_g(2, True, range(3, len(pieces)))

    for way in range(2):
        @pl.when(passes(way))
        def _(way=way):
            for q in range(it_sent, parts):
                copy_z(q, way, 0, o).start()

    @pl.when(middle)
    def _():
        copy_e(0, 0, across).wait_recv()
        copy_e(1, 0, across).start()

    fetch.wait()
    tell.wait()
    for way in range(2):
        @pl.when(ends_at(way))
        def _(way=way):
            for hop in range(last - 1):
                for n in range(len(pieces)):
                    got_g(n, way, hop).wait_recv()
                    flip(held(way, hop + 1), n)

    far_plane = (1 - upper) * last
    count = len(pieces)
    for span in (range(count - 2), range(count - 2, count - 1), range(count - 1, count)):
        for n in span:
            for way in range(2):
                @pl.when(ends_at(way))
                def _(way=way, n=n):
                    got_g(n, way, last - 1).wait_recv()

            flip(far_plane, n)

        def rows_step(r, carry, span=span):
            for pair in (2 * r, 2 * r + 1):
                left = jnp.concatenate([coef[2 * pair], coef[2 * pair + 1]])
                for n in span:
                    first, size = pieces[n]
                    made = jnp.dot(
                        left, flat[:, first:first + size], preferred_element_type=f32
                    ).astype(bf16)
                    y_rows[2 * pair, :, first:first + size] = made[:TILE]
                    y_rows[2 * pair + 1, :, first:first + size] = made[TILE:]
            return carry

        lax.fori_loop(0, coef.shape[0] // 4, rows_step, 0)

    for way in range(2):
        @pl.when(passes(1 - way))
        def _(way=way):
            each_part(lambda q: copy_z(q, way, 0, o).start())

    for way in range(2):
        @pl.when(passes(way))
        def _(way=way):
            def on(q):
                copy_z(q, way, 0, held(way, 1)).wait_recv()
                copy_z(q, way, 1, held(way, 1)).start()

            each_part(on)

    @pl.when(middle)
    def _():
        copy_e(2, 0, other_core).start()
        copy_e(1, 1, across).wait_recv()
        copy_e(3, 1, other_core).start()

    drain(0, parts)

    def place(block, panel, j, k):
        code = code_of[block * n_pan + j, SCAP * panel + k]
        kept = lax.shift_right_logical(code, 12)
        row = lax.shift_right_logical(code - kept * KEPT_CODE, 6)
        return row, code - kept * KEPT_CODE - row * ROW_CODE, kept.astype(f32)

    def tile_part(panel, j, k):
        row, col, kept = place(0, panel, j, k)
        return jnp.dot(y_rows[row], virt[panel, col], preferred_element_type=f32) * kept

    def tile_rest(it, carry):
        @pl.when((it >= LAGS[1]) & (it < pairs + LAGS[1]))
        def _():
            second(it - LAGS[1], parts)

        @pl.when(it >= LAGS[2])
        def _():
            pair = it - LAGS[2]

            def store(h, t, tile):
                done[2 * pair + t, h] = tile

            third(pair, parts, store)

        return carry

    def tile_step(it, carry):
        @pl.when(it < pairs)
        def _():
            def one(g, c):
                for k in range(SCAP):
                    for t in range(2):
                        made = tile_part(2 * it + t, 2 * g + 1 - core, k)
                        send_c[
                            it, g, k * TILE:(k + 1) * TILE, t * TILE:(t + 1) * TILE
                        ] = made.astype(bf16)
                return c

            for g in range(group):
                one(g, 0)
            copy_c(it, parts).start()

        @pl.when((it >= LAGS[0]) & (it < pairs + LAGS[0]))
        def _():
            pair = it - LAGS[0]
            ch = parts + pair
            copy_c(pair, parts).wait_recv()
            for b, a in ((1, 1), (0, 1), (1, 0), (0, 0)):
                g = near(b, a)
                j = 2 * g + core
                for k in range(SCAP):
                    for t in range(2):
                        rows = slice(k * TILE, (k + 1) * TILE)
                        cols = slice(t * TILE, (t + 1) * TILE)
                        total = tile_part(2 * pair + t, j, k)
                        total = total + recv_c[ch, g, rows, cols].astype(f32)
                        if k == 0 and a:
                            send_a[pair, b, :, cols] = total.astype(bf16)
                        elif k == 0:
                            keep_a[pair, b, :, cols] = total
                        elif b:
                            send_b[pair, a, :, cols] = total.astype(bf16)
                        else:
                            keep_b[pair, a, :, cols] = total
                if (b, a) == (0, 1):
                    copy_a(pair, parts).start()
                if (b, a) == (1, 0):
                    copy_b(pair, parts).start()

        return tile_rest(it, carry)

    lax.fori_loop(0, pairs + LAGS[0], tile_step, 0)

    def copy_f(j):
        return remote(send_f.at[j], recv_f.at[j], f_out.at[j], f_in.at[j], s, upper * last)

    @pl.when(middle)
    def _():
        for way in range(2):
            @pl.when(passes(1 - way))
            def _(way=way):
                each_part(lambda q: copy_z(q, way, 0, held(way, 1)).wait_recv())
                each_part(lambda q: copy_z(q, way, 1, held(way, 2)).wait_recv())

        copy_e(2, 0, other_core).wait_recv()
        copy_e(3, 1, other_core).wait_recv()
        far = 2 - 2 * upper

        def far_owner(d, c):
            j = lax.rem(s + d, n_pan)
            for k in range(SCAP):
                row, col, kept = place(1, s, j, k)
                total = jnp.dot(
                    coef_far[row],
                    jnp.concatenate([whole[far + z, col] for z in range(2)]),
                    preferred_element_type=f32,
                )
                send_f[j, k] = (total * kept).astype(bf16)
            copy_f(j).start()
            return c

        lax.fori_loop(1, n_pan + 1, far_owner, 0)

    lax.fori_loop(pairs + LAGS[0], pairs + LAGS[1], tile_rest, 0)
    for way, end in ((1, 0), (0, last)):
        @pl.when(o == end)
        def _(way=way, end=end):
            each_part(lambda q: copy_z(q, way, 0, held(way, 1)).wait_recv())
            first = 0 if end == 0 else n_occ - 2

            def near_owner(j, c):
                for k in range(SCAP):
                    row, col, kept = place(0, s, j, k)
                    total = jnp.dot(
                        coef[row, :, first * half:(first + 2) * half],
                        jnp.concatenate([whole[first + z, col] for z in range(2)]),
                        preferred_element_type=f32,
                    )
                    near_f[j, k] = total * kept
                return c

            lax.fori_loop(0, n_pan, near_owner, 0)

    finished = pltpu.make_async_copy(done, out_ref.at[:, :, 0], done_sem)

    def tile_send(d, source, target):
        return remote(
            picked.at[target], out_ref.at[source, :, 1], t_out.at[d - 1], t_in.at[d - 1], target
        )

    own = pltpu.make_async_copy(picked.at[s], out_ref.at[s, :, 1], own_sem)

    def give(d, j):
        @pl.when(d < n_pan)
        def _():
            tile_send(d, s, j).start()

        @pl.when(d == n_pan)
        def _():
            own.start()

    @pl.when(middle)
    def _():
        def one_owner(d, c):
            j = lax.rem(s + d, n_pan)
            for k in range(SCAP):
                row, col, kept = place(0, s, j, k)
                total = jnp.dot(
                    coef[row],
                    jnp.concatenate([whole[z, col] for z in range(n_occ)]),
                    preferred_element_type=f32,
                )
                picked[j, k] = (total * kept).astype(bf16)
            give(d, j)
            return c

        lax.fori_loop(1, n_pan + 1, one_owner, 0)

    @pl.when(~middle)
    def _():
        def one_owner(d, c):
            j = lax.rem(s + d, n_pan)
            copy_f(j).wait_recv()
            for k in range(SCAP):
                picked[j, k] = (near_f[j, k] + recv_f[j, k].astype(f32)).astype(bf16)
            give(d, j)
            return c

        lax.fori_loop(1, n_pan - 2, one_owner, 0)
        lax.fori_loop(pairs + LAGS[1], pairs + LAGS[2], tile_rest, 0)
        finished.start()
        lax.fori_loop(n_pan - 2, n_pan + 1, one_owner, 0)

    for end in (0, last):
        @pl.when(o == end)
        def _(end=end):
            copy_e0(end).wait_send()

    @pl.when(middle)
    def _():
        lax.fori_loop(pairs + LAGS[1], pairs + LAGS[2], tile_rest, 0)
        finished.start()
        copy_e(1, 0, across).wait_send()
        copy_e(2, 0, other_core).wait_send()
        copy_e(3, 1, other_core).wait_send()

        def sent(j, c):
            copy_f(j).wait_send()
            return c

        lax.fori_loop(0, n_pan, sent, 0)

    drain(parts, pairs)

    for way in range(2):
        for hop in range(last):
            @pl.when(sends(way, hop))
            def _(hop=hop, way=way):
                for n in range(len(pieces)):
                    copy_g(n, way, hop).wait_send()

        @pl.when(sends(way, 0))
        def _(way=way):
            each_part(lambda q: copy_z(q, way, 0, o).wait_send())

        @pl.when(passes(way))
        def _(way=way):
            each_part(lambda q: copy_z(q, way, 1, held(way, 1)).wait_send())

    def finish(d, c):
        tile_send(d, s, lax.rem(s + d, n_pan)).wait_send()
        source = lax.rem(s + n_pan - d, n_pan)
        tile_send(d, source, source).wait_recv()
        return c

    lax.fori_loop(1, n_pan, finish, 0)
    finished.wait()
    own.wait()


def by_kernel(n_occ, n_pan, gamma_ia, coef_virt, coef_occ, tile_mask, tile_owner):
    half = gamma_ia.shape[1]
    depth = gamma_ia.shape[2]
    panel_width = coef_virt.shape[0] // n_pan
    row_tiles = coef_occ.shape[0] // TILE
    col_tiles = panel_width // TILE
    parts = col_tiles // 2
    width = 2 * TILE
    pairs = n_pan // 2
    chunks = parts + pairs
    most = max(parts, pairs)
    group = n_pan // 2
    quarter = half // 2
    far = 2 * half
    bf16, f32 = jnp.bfloat16, jnp.float32
    dma = pltpu.SemaphoreType.DMA
    hbm = pl.BlockSpec(memory_space=pl.ANY)
    vmem = pl.BlockSpec(memory_space=pltpu.VMEM)
    pieces = len(pieces_of(depth))
    arrived = pl.pallas_call(
        functools.partial(kernel, n_occ, n_pan, parts),
        out_shape=pltpu.VMEM((n_pan, SCAP, AUX, TILE, TILE), bf16),
        in_specs=[vmem, vmem, hbm, hbm, hbm],
        out_specs=hbm,
        scratch_shapes=[
            pltpu.VMEM((n_occ, depth, half), bf16),
            pltpu.VMEM((n_occ * half, depth), bf16),
            pltpu.VMEM((depth, half), bf16),
            pltpu.VMEM((half, depth), bf16),
            pltpu.VMEM((n_pan, col_tiles, depth, TILE), bf16),
            pltpu.VMEM((row_tiles, TILE, coef_occ.shape[1]), bf16),
            pltpu.VMEM((row_tiles, TILE, depth), bf16),
            pltpu.VMEM((most, group, half, width), bf16),
            pltpu.VMEM((chunks, group, half, width), bf16),
            pltpu.VMEM((most, 2, quarter, width), f32),
            pltpu.VMEM((most, 2, quarter, width), f32),
            pltpu.VMEM((most, 2, quarter, width), bf16),
            pltpu.VMEM((chunks, 2, quarter, width), bf16),
            pltpu.VMEM((most, 2, quarter, width), bf16),
            pltpu.VMEM((chunks, 2, quarter, width), bf16),
            pltpu.VMEM((most, quarter, width), bf16),
            pltpu.VMEM((chunks, quarter, width), bf16),
            pltpu.VMEM((most, quarter, width), bf16),
            pltpu.VMEM((chunks, quarter, width), bf16),
            pltpu.VMEM((n_occ, col_tiles, half, TILE), bf16),
            pltpu.VMEM((n_pan, SCAP, TILE, TILE), bf16),
            pltpu.VMEM((n_pan, SCAP, TILE, TILE), bf16),
            pltpu.VMEM((row_tiles, TILE, far), bf16),
            pltpu.VMEM((n_pan, SCAP, TILE, TILE), bf16),
            pltpu.VMEM((n_pan, SCAP, TILE, TILE), bf16),
            pltpu.VMEM((n_pan, SCAP, TILE, TILE), f32),
            pltpu.VMEM((2 * n_pan, TILE), jnp.int32),
            pltpu.SMEM((2 * n_pan, TILE), jnp.int32),
            dma,
            dma((n_pan, col_tiles)), dma, dma, dma, dma, dma,
            *[dma((chunks,)) for _ in range(10)],
            dma((2, n_occ - 1, pieces)), dma((2, n_occ - 1, pieces)),
            dma((2, 2, parts)), dma((2, 2, parts)),
            dma((n_pan - 1,)), dma((n_pan - 1,)),
            dma((4,)), dma((4,)), dma((n_pan,)), dma((n_pan,)),
        ],
        compiler_params=pltpu.CompilerParams(
            collective_id=0, has_side_effects=True, vmem_limit_bytes=65000000
        ),
    )(
        tile_mask,
        tile_owner,
        jnp.swapaxes(gamma_ia, 1, 2),
        coef_virt.T,
        coef_occ.reshape(row_tiles, TILE, coef_occ.shape[1]),
    )
    return arrived[None, None]


def solution(mesh):
    n_occ, n_pan = mesh.shape["occ"], mesh.shape["pan"]

    def local(gamma_ia, coef_virt, coef_occ, tile_mask, tile_owner):
        fits = (
            n_occ == 4
            and n_pan == 8
            and gamma_ia.shape[1] == 2 * TILE
            and gamma_ia.shape[2] >= PIECE
            and coef_virt.shape[0] % (2 * TILE * n_pan) == 0
            and coef_occ.shape[0] % (4 * TILE) == 0
        )
        if fits:
            return by_kernel(n_occ, n_pan, gamma_ia, coef_virt, coef_occ, tile_mask, tile_owner)
        return by_collectives(gamma_ia, coef_virt, coef_occ, tile_mask, tile_owner)

    return jax.shard_map(
        local,
        mesh=mesh,
        in_specs=(P(None, "occ", "pan"), P(None, "pan"), P("occ", None), P(), P()),
        out_specs=P("occ", "pan", None, None, None, None, None),
        check_vma=False,
    )
```

```python
import functools

import jax
import jax.numpy as jnp
from jax import lax
from jax.experimental import pallas as pl
from jax.experimental.pallas import tpu as pltpu
from jax.sharding import PartitionSpec as P

AUX = 2
TILE = 128
SCAP = 2
PIECE = 256
LAGS = (1, 3, 5)
ROW_CODE = 64
KEPT_CODE = 4096
MESH = pl.DeviceIdType.MESH


def find_codes(blocks, mask, owner_in, row_tiles, col_tiles, owners):
    col = lax.broadcasted_iota(jnp.int32, mask.shape, 1)
    owner = jnp.where(mask == 1, owner_in, -1)
    codes = []
    for block in blocks:
        row = lax.broadcasted_iota(jnp.int32, mask.shape, 0) - block * row_tiles
        owner_of = jnp.where((row >= 0) & (row < row_tiles), owner, -1)
        place = row * ROW_CODE + col
        least, most = [], []
        for j in range(owners):
            chosen = owner_of == j
            least.append(jnp.min(jnp.where(chosen, place, 1 << 20), axis=0, keepdims=True))
            most.append(jnp.max(jnp.where(chosen, place, -1), axis=0, keepdims=True))
        least, most = jnp.concatenate(least), jnp.concatenate(most)
        lane = lax.broadcasted_iota(jnp.int32, least.shape, 1)
        slot = lax.broadcasted_iota(jnp.int32, (owners, TILE), 1)
        code = jnp.zeros((owners, TILE), jnp.int32)
        for s in range(owners):
            mine = (lane >= s * col_tiles) & (lane < (s + 1) * col_tiles)
            low = jnp.min(jnp.where(mine, least, 1 << 20), axis=1, keepdims=True)
            high = jnp.max(jnp.where(mine, most, -1), axis=1, keepdims=True)
            shift = KEPT_CODE - s * col_tiles
            code = jnp.where(slot == SCAP * s, jnp.where(high >= 0, low + shift, 0), code)
            code = jnp.where(slot == SCAP * s + 1, jnp.where(high > low, high + shift, 0), code)
        codes.append(code)
    return jnp.concatenate(codes)


def by_collectives(gamma_ia, coef_virt, coef_occ, tile_mask, tile_owner):
    panels = lax.axis_size("pan")
    occ_local = gamma_ia.shape[1]
    panel_width = coef_virt.shape[0] // panels
    row_tiles = coef_occ.shape[0] // TILE
    col_tiles = panel_width // TILE
    gamma_flat = gamma_ia.reshape(AUX * occ_local, gamma_ia.shape[2])
    summed = lax.psum_scatter(
        lax.dot_general(
            coef_virt, gamma_flat, (((1,), (1,)), ((), ())), preferred_element_type=jnp.float32
        ),
        "pan",
        scatter_dimension=0,
        tiled=True,
    )
    half_x = summed.astype(jnp.bfloat16).reshape(panel_width, AUX, occ_local)
    whole_x = lax.all_gather(half_x, "occ", axis=2, tiled=True)
    codes = find_codes(
        [lax.axis_index("occ")], tile_mask, tile_owner, row_tiles, col_tiles, panels
    )
    codes = lax.dynamic_slice(codes, (0, lax.axis_index("pan") * SCAP), (panels, SCAP)).reshape(-1)
    filled = codes // KEPT_CODE
    row = codes % KEPT_CODE // ROW_CODE
    col = codes % ROW_CODE
    bf16 = jnp.bfloat16
    row_pick = (row[:, None] == jnp.arange(row_tiles)[None, :]).astype(bf16)
    col_pick = (col[:, None] == jnp.arange(col_tiles)[None, :]).astype(bf16)
    row_set = jnp.einsum(
        "st,tri->sri", row_pick, coef_occ.reshape(row_tiles, TILE, coef_occ.shape[1])
    )
    col_set = jnp.einsum(
        "st,tkpi->skpi", col_pick, whole_x.reshape(col_tiles, TILE, AUX, whole_x.shape[2])
    )
    picked = jnp.einsum("sri,skpi->sprk", row_set, col_set, preferred_element_type=jnp.float32)
    picked = (
        picked.reshape(panels, SCAP, AUX, TILE, TILE)
        * filled.astype(jnp.float32).reshape(panels, SCAP)[:, :, None, None, None]
    )
    arrived = lax.all_to_all(
        picked.astype(jnp.bfloat16), "pan", split_axis=0, concat_axis=0, tiled=True
    )
    return arrived[None, None]


def pieces_of(depth):
    later = depth // PIECE - 1
    first = (depth - later * PIECE + TILE) // TILE * TILE
    starts = [0] + [first + n * PIECE for n in range(later)] + [depth]
    return [(a, b - a) for a, b in zip(starts[:-1], starts[1:])]


def kernel(
    n_occ, n_pan, parts,
    mask_ref, owner_ref, gamma_ref, virt_ref, occ_ref, out_ref,
    gam, flat, stage, gam_1, virt, coef, y_rows, send_c, recv_c, keep_a, keep_b,
    send_a, recv_a, send_b, recv_b, send_2a, recv_2a, send_2b, recv_2b,
    whole, picked, done, coef_far, send_f, recv_f, near_f, code_in, code_of, code_sem,
    load_sem, coef_sem, own_sem, done_sem, gam_sem, stage_sem,
    c_out, c_in, a_out, a_in, b_out, b_in, a2_out, a2_in, b2_out, b2_in,
    g_out, g_in, z_out, z_in, t_out, t_in, e_out, e_in, f_out, f_in,
):
    o = lax.axis_index("occ")
    s = lax.axis_index("pan")
    core = lax.rem(s, 2)
    x = lax.rem(s // 2, 2)
    y = s // 4
    other_core = s + 1 - 2 * core
    other_x = s + 2 - 4 * x
    other_y = s + 4 - 8 * y
    group = n_pan // 2
    half, depth = gam_1.shape
    quarter = half // 2
    tiles = half // TILE
    pairs = n_pan // 2
    last = n_occ - 1
    upper = o // 2
    middle = (o > 0) & (o < last)
    bf16, f32 = jnp.bfloat16, jnp.float32
    pieces = pieces_of(depth)

    def load(pan, t):
        first = pl.multiple_of((pan * (parts * tiles) + t) * TILE, TILE)
        return pltpu.make_async_copy(
            virt_ref.at[:, pl.ds(first, TILE)], virt.at[pan, t], load_sem.at[pan, t]
        )

    def load_part(q):
        for g in range(group):
            for t in range(tiles):
                load(2 * g + 1 - core, q * tiles + t).start()
        for g in range(group):
            for t in range(tiles):
                load(2 * g + core, q * tiles + t).start()

    take_0 = pltpu.make_async_copy(gamma_ref.at[0], gam.at[o], gam_sem)
    take_1 = pltpu.make_async_copy(gamma_ref.at[1], stage, stage_sem)
    fetch = pltpu.make_async_copy(occ_ref, coef, coef_sem)
    tell = pltpu.make_async_copy(code_in, code_of, code_sem)
    take_1.start()

    barrier = pltpu.get_barrier_semaphore()
    for d in range(1, n_pan):
        pl.semaphore_signal(
            barrier, inc=1, device_id=(o, lax.rem(s + d, n_pan)), device_id_type=MESH
        )
    for d in range(1, n_occ):
        pl.semaphore_signal(
            barrier, inc=1, device_id=(lax.rem(o + d, n_occ), s), device_id_type=MESH
        )
    load_part(0)
    take_0.start()
    pl.semaphore_wait(barrier, n_pan + n_occ - 2)

    def remote(src, dst, out_sem, in_sem, pan, row=None):
        return pltpu.make_async_remote_copy(
            src_ref=src, dst_ref=dst, send_sem=out_sem, recv_sem=in_sem,
            device_id=(o if row is None else row, pan), device_id_type=MESH,
        )

    def copy_c(n, base):
        ch = base + n
        return remote(send_c.at[n], recv_c.at[ch], c_out.at[ch], c_in.at[ch], other_core)

    def copy_a(n, base):
        ch = base + n
        return remote(send_a.at[n], recv_a.at[ch], a_out.at[ch], a_in.at[ch], other_x)

    def copy_b(n, base):
        ch = base + n
        return remote(send_b.at[n], recv_b.at[ch], b_out.at[ch], b_in.at[ch], other_y)

    def copy_2a(n, base):
        ch = base + n
        return remote(send_2a.at[n], recv_2a.at[ch], a2_out.at[ch], a2_in.at[ch], other_y)

    def copy_2b(n, base):
        ch = base + n
        return remote(send_2b.at[n], recv_2b.at[ch], b2_out.at[ch], b2_in.at[ch], other_x)

    def drain(base, count):
        def one(n, c):
            for copy in (copy_c, copy_a, copy_b, copy_2a, copy_2b):
                copy(n, base).wait_send()
            return c

        lax.fori_loop(0, count, one, 0)

    def beyond(way):
        return jnp.clip(o + 1 - 2 * way, 0, last)

    def held(way, hop):
        return o - hop if way == 0 else o + hop

    def sends(way, hop):
        return (o < last) & (o >= hop) if way == 0 else (o > 0) & (o + hop <= last)

    def passes(way):
        return o == 1 if way == 0 else o == last - 1

    def ends_at(way):
        return o == last if way == 0 else o == 0

    def copy_g(n, way, hop):
        first, size = pieces[n]
        part = gam.at[held(way, hop), pl.ds(first, size)]
        mine = gamma_ref.at[0, pl.ds(first, size)]
        return remote(
            mine if hop == 0 else part, part,
            g_out.at[way, hop, n], g_in.at[way, hop, n], s, beyond(way),
        )

    def got_g(n, way, hop):
        first, size = pieces[n]
        part = gam.at[held(way, hop + 1), pl.ds(first, size)]
        return remote(
            part, part, g_out.at[way, hop, n], g_in.at[way, hop, n], s, beyond(way)
        )

    def pass_g(hop, when=True, some=range(len(pieces))):
        for way in range(2):
            @pl.when(sends(way, hop) & when)
            def _(way=way):
                for n in some:
                    if hop:
                        got_g(n, way, hop - 1).wait_recv()
                    copy_g(n, way, hop).start()

    def flip(z, n):
        first, size = pieces[n]
        rows = pl.ds(pl.multiple_of(z * half, half), half)
        flat[rows, first:first + size] = gam[z, first:first + size].T

    def copy_z(q, way, hop, source):
        part = whole.at[source, pl.ds(q * tiles, tiles)]
        return remote(
            part, part, z_out.at[way, hop, q], z_in.at[way, hop, q], s, beyond(way)
        )

    def each_part(todo):
        def one(q, c):
            todo(q)
            return c

        lax.fori_loop(0, parts, one, 0)

    parity = x + y - 2 * x * y
    some = coef.shape[0] // 4
    cols = 2 * half

    def band(odd):
        return pl.ds((2 * (parity + odd - 2 * parity * odd) + core) * some, some)

    def copy_e0(end):
        first = cols if end == 0 else 0
        return remote(
            occ_ref.at[band(0), :, pl.ds(first, cols)], coef_far.at[band(0)],
            e_out.at[0], e_in.at[0], s, 1 if end == 0 else last - 1,
        )

    def copy_e(step, odd, pan):
        return remote(
            coef_far.at[band(odd)], coef_far.at[band(odd)], e_out.at[step], e_in.at[step], pan
        )

    across = other_x + core * (other_y - other_x)

    pass_g(0)
    for end in (0, last):
        @pl.when(o == end)
        def _(end=end):
            copy_e0(end).start()

    take_1.wait()
    gam_1[...] = stage[...].T

    def second(n, base):
        ch = base + n
        copy_a(n, base).wait_recv()
        send_2a[n] = (keep_a[n, 1] + recv_a[ch, 1].astype(f32)).astype(bf16)
        copy_2a(n, base).start()
        copy_b(n, base).wait_recv()
        send_2b[n] = (keep_b[n, 1] + recv_b[ch, 1].astype(f32)).astype(bf16)
        copy_2b(n, base).start()
        keep_a[n, 0] = keep_a[n, 0] + recv_a[ch, 0].astype(f32)
        keep_b[n, 0] = keep_b[n, 0] + recv_b[ch, 0].astype(f32)

    def third(n, base, store):
        ch = base + n
        copy_2a(n, base).wait_recv()
        copy_2b(n, base).wait_recv()
        for h, keep, arrived in ((0, keep_a, recv_2a), (1, keep_b, recv_2b)):
            total = (keep[n, 0] + arrived[ch].astype(f32)).astype(bf16)
            for t in range(tiles):
                store(h, t, total[:, t * TILE:(t + 1) * TILE])

    def near(b, a):
        return (y + b - 2 * y * b) * 2 + x + a - 2 * x * a

    def product(q, pan):
        columns = jnp.concatenate([virt[pan, q * tiles + t] for t in range(tiles)], axis=1)
        return jnp.dot(gam_1[...], columns, preferred_element_type=f32)

    it_sent = max(parts - 2, 0)

    def half_step(it, carry):
        @pl.when(it + 1 < parts)
        def _():
            load_part(it + 1)

        @pl.when(it == parts)
        def _():
            fetch.start()

        @pl.when(it < parts)
        def _():
            for g in range(group):
                for t in range(tiles):
                    load(2 * g + 1 - core, it * tiles + t).wait()

            def one(g, c):
                send_c[it, g] = product(it, 2 * g + 1 - core).astype(bf16)
                return c

            for g in range(group):
                one(g, 0)
            copy_c(it, 0).start()

        @pl.when((it >= LAGS[0]) & (it < parts + LAGS[0]))
        def _():
            q = it - LAGS[0]
            for g in range(group):
                for t in range(tiles):
                    load(2 * g + core, q * tiles + t).wait()
            copy_c(q, 0).wait_recv()
            for b, a in ((1, 1), (0, 1), (1, 0), (0, 0)):
                g = near(b, a)
                total = product(q, 2 * g + core) + recv_c[q, g].astype(f32)
                if a:
                    send_a[q, b] = total[:quarter].astype(bf16)
                else:
                    keep_a[q, b] = total[:quarter]
                if b:
                    send_b[q, a] = total[quarter:].astype(bf16)
                else:
                    keep_b[q, a] = total[quarter:]
                if (b, a) == (0, 1):
                    copy_a(q, 0).start()
                if (b, a) == (1, 0):
                    copy_b(q, 0).start()

        pass_g(1, it == 3, (0, 1))
        pass_g(1, it == 5, range(2, len(pieces)))

        @pl.when((it >= LAGS[1]) & (it < parts + LAGS[1]))
        def _():
            second(it - LAGS[1], 0)

        @pl.when(it >= LAGS[2])
        def _():
            q = it - LAGS[2]

            def store(h, t, tile):
                whole[o, q * tiles + t, h * quarter:(h + 1) * quarter] = tile

            third(q, 0, store)
            for end, way in ((0, 0), (last, 1)):
                @pl.when(o == end)
                def _(way=way):
                    copy_z(q, way, 0, o).start()

        for way in range(2):
            @pl.when(passes(way) & (it == parts + 3))
            def _(way=way):
                for q in range(it_sent):
                    copy_z(q, way, 0, o).start()

        @pl.when(it == parts)
        def _():
            code_in[...] = find_codes(
                [o, upper * last], mask_ref[...], owner_ref[...],
                coef.shape[0], parts * tiles, n_pan,
            )
            tell.start()
            take_0.wait()
            for n in range(len(pieces)):
                flip(o, n)

        pass_g(2, it == parts + 2, (0, 1))
        pass_g(2, it == parts + 3, (2,))

        for side in (-1, 1):
            @pl.when(middle & (it == parts + 1))
            def _(side=side):
                for n in range(len(pieces)):
                    flip(o + side, n)

        return carry

    lax.fori_loop(0, parts + LAGS[2], half_step, 0)

    pass_g(2, True, range(3, len(pieces)))

    for way in range(2):
        @pl.when(passes(way))
        def _(way=way):
            for q in range(it_sent, parts):
                copy_z(q, way, 0, o).start()

    @pl.when(middle)
    def _():
        copy_e(0, 0, across).wait_recv()
        copy_e(1, 0, across).start()

    fetch.wait()
    tell.wait()
    for way in range(2):
        @pl.when(ends_at(way))
        def _(way=way):
            for hop in range(last - 1):
                for n in range(len(pieces)):
                    got_g(n, way, hop).wait_recv()
                    flip(held(way, hop + 1), n)

    far_plane = (1 - upper) * last
    count = len(pieces)
    per_step = 5 if coef.shape[0] // 2 % 5 == 0 else 2
    for span in (range(count - 2), range(count - 2, count - 1), range(count - 1, count)):
        for n in span:
            for way in range(2):
                @pl.when(ends_at(way))
                def _(way=way, n=n):
                    got_g(n, way, last - 1).wait_recv()

            flip(far_plane, n)

        def rows_step(r, carry, span=span):
            for n in range(per_step):
                pair = per_step * r + n
                left = jnp.concatenate([coef[2 * pair], coef[2 * pair + 1]])
                for m in span:
                    first, size = pieces[m]
                    made = jnp.dot(
                        left, flat[:, first:first + size], preferred_element_type=f32
                    ).astype(bf16)
                    y_rows[2 * pair, :, first:first + size] = made[:TILE]
                    y_rows[2 * pair + 1, :, first:first + size] = made[TILE:]
            return carry

        lax.fori_loop(0, coef.shape[0] // 2 // per_step, rows_step, 0)

    for way in range(2):
        @pl.when(passes(1 - way))
        def _(way=way):
            each_part(lambda q: copy_z(q, way, 0, o).start())

    for way in range(2):
        @pl.when(passes(way))
        def _(way=way):
            def on(q):
                copy_z(q, way, 0, held(way, 1)).wait_recv()
                copy_z(q, way, 1, held(way, 1)).start()

            each_part(on)

    @pl.when(middle)
    def _():
        copy_e(2, 0, other_core).start()
        copy_e(1, 1, across).wait_recv()
        copy_e(3, 1, other_core).start()

    drain(0, parts)

    def place(block, panel, j, k):
        code = code_of[block * n_pan + j, SCAP * panel + k]
        kept = lax.shift_right_logical(code, 12)
        row = lax.shift_right_logical(code - kept * KEPT_CODE, 6)
        return row, code - kept * KEPT_CODE - row * ROW_CODE, kept.astype(f32)

    def tile_part(panel, j, k):
        row, col, kept = place(0, panel, j, k)
        return jnp.dot(y_rows[row], virt[panel, col], preferred_element_type=f32) * kept

    def tile_rest(it, carry):
        @pl.when((it >= LAGS[1]) & (it < pairs + LAGS[1]))
        def _():
            second(it - LAGS[1], parts)

        @pl.when(it >= LAGS[2])
        def _():
            pair = it - LAGS[2]

            def store(h, t, tile):
                done[2 * pair + t, h] = tile

            third(pair, parts, store)

        return carry

    def tile_step(it, carry):
        @pl.when(it < pairs)
        def _():
            def one(g, c):
                for k in range(SCAP):
                    for t in range(2):
                        made = tile_part(2 * it + t, 2 * g + 1 - core, k)
                        send_c[
                            it, g, k * TILE:(k + 1) * TILE, t * TILE:(t + 1) * TILE
                        ] = made.astype(bf16)
                return c

            for g in range(group):
                one(g, 0)
            copy_c(it, parts).start()

        @pl.when((it >= LAGS[0]) & (it < pairs + LAGS[0]))
        def _():
            pair = it - LAGS[0]
            ch = parts + pair
            copy_c(pair, parts).wait_recv()
            for b, a in ((1, 1), (0, 1), (1, 0), (0, 0)):
                g = near(b, a)
                j = 2 * g + core
                for k in range(SCAP):
                    for t in range(2):
                        rows = slice(k * TILE, (k + 1) * TILE)
                        cols = slice(t * TILE, (t + 1) * TILE)
                        total = tile_part(2 * pair + t, j, k)
                        total = total + recv_c[ch, g, rows, cols].astype(f32)
                        if k == 0 and a:
                            send_a[pair, b, :, cols] = total.astype(bf16)
                        elif k == 0:
                            keep_a[pair, b, :, cols] = total
                        elif b:
                            send_b[pair, a, :, cols] = total.astype(bf16)
                        else:
                            keep_b[pair, a, :, cols] = total
                if (b, a) == (0, 1):
                    copy_a(pair, parts).start()
                if (b, a) == (1, 0):
                    copy_b(pair, parts).start()

        return tile_rest(it, carry)

    lax.fori_loop(0, pairs + LAGS[0], tile_step, 0)

    def copy_f(j):
        return remote(send_f.at[j], recv_f.at[j], f_out.at[j], f_in.at[j], s, upper * last)

    @pl.when(middle)
    def _():
        for way in range(2):
            @pl.when(passes(1 - way))
            def _(way=way):
                each_part(lambda q: copy_z(q, way, 0, held(way, 1)).wait_recv())
                each_part(lambda q: copy_z(q, way, 1, held(way, 2)).wait_recv())

        copy_e(2, 0, other_core).wait_recv()
        copy_e(3, 1, other_core).wait_recv()
        far = 2 - 2 * upper

        def far_owner(d, c):
            j = lax.rem(s + d, n_pan)
            for k in range(SCAP):
                row, col, kept = place(1, s, j, k)
                total = jnp.dot(
                    coef_far[row],
                    jnp.concatenate([whole[far + z, col] for z in range(2)]),
                    preferred_element_type=f32,
                )
                send_f[j, k] = (total * kept).astype(bf16)
            copy_f(j).start()
            return c

        lax.fori_loop(1, n_pan + 1, far_owner, 0)

    lax.fori_loop(pairs + LAGS[0], pairs + LAGS[1], tile_rest, 0)
    for way, end in ((1, 0), (0, last)):
        @pl.when(o == end)
        def _(way=way, end=end):
            each_part(lambda q: copy_z(q, way, 0, held(way, 1)).wait_recv())
            first = 0 if end == 0 else n_occ - 2

            def near_owner(j, c):
                for k in range(SCAP):
                    row, col, kept = place(0, s, j, k)
                    total = jnp.dot(
                        coef[row, :, first * half:(first + 2) * half],
                        jnp.concatenate([whole[first + z, col] for z in range(2)]),
                        preferred_element_type=f32,
                    )
                    near_f[j, k] = total * kept
                return c

            lax.fori_loop(0, n_pan, near_owner, 0)

    finished = pltpu.make_async_copy(done, out_ref.at[:, :, 0], done_sem)

    def tile_send(d, source, target):
        return remote(
            picked.at[target], out_ref.at[source, :, 1], t_out.at[d - 1], t_in.at[d - 1], target
        )

    own = pltpu.make_async_copy(picked.at[s], out_ref.at[s, :, 1], own_sem)

    def give(d, j):
        @pl.when(d < n_pan)
        def _():
            tile_send(d, s, j).start()

        @pl.when(d == n_pan)
        def _():
            own.start()

    @pl.when(middle)
    def _():
        def one_owner(d, c):
            j = lax.rem(s + d, n_pan)
            for k in range(SCAP):
                row, col, kept = place(0, s, j, k)
                total = jnp.dot(
                    coef[row],
                    jnp.concatenate([whole[z, col] for z in range(n_occ)]),
                    preferred_element_type=f32,
                )
                picked[j, k] = (total * kept).astype(bf16)
            give(d, j)
            return c

        lax.fori_loop(1, n_pan + 1, one_owner, 0)

    @pl.when(~middle)
    def _():
        def one_owner(d, c):
            j = lax.rem(s + d, n_pan)
            copy_f(j).wait_recv()
            for k in range(SCAP):
                picked[j, k] = (near_f[j, k] + recv_f[j, k].astype(f32)).astype(bf16)
            give(d, j)
            return c

        lax.fori_loop(1, n_pan - 2, one_owner, 0)
        lax.fori_loop(pairs + LAGS[1], pairs + LAGS[2], tile_rest, 0)
        finished.start()
        lax.fori_loop(n_pan - 2, n_pan + 1, one_owner, 0)

    for end in (0, last):
        @pl.when(o == end)
        def _(end=end):
            copy_e0(end).wait_send()

    @pl.when(middle)
    def _():
        lax.fori_loop(pairs + LAGS[1], pairs + LAGS[2], tile_rest, 0)
        finished.start()
        copy_e(1, 0, across).wait_send()
        copy_e(2, 0, other_core).wait_send()
        copy_e(3, 1, other_core).wait_send()

        def sent(j, c):
            copy_f(j).wait_send()
            return c

        lax.fori_loop(0, n_pan, sent, 0)

    drain(parts, pairs)

    for way in range(2):
        for hop in range(last):
            @pl.when(sends(way, hop))
            def _(hop=hop, way=way):
                for n in range(len(pieces)):
                    copy_g(n, way, hop).wait_send()

        @pl.when(sends(way, 0))
        def _(way=way):
            each_part(lambda q: copy_z(q, way, 0, o).wait_send())

        @pl.when(passes(way))
        def _(way=way):
            each_part(lambda q: copy_z(q, way, 1, held(way, 1)).wait_send())

    def finish(d, c):
        tile_send(d, s, lax.rem(s + d, n_pan)).wait_send()
        source = lax.rem(s + n_pan - d, n_pan)
        tile_send(d, source, source).wait_recv()
        return c

    lax.fori_loop(1, n_pan, finish, 0)
    finished.wait()
    own.wait()


def by_kernel(n_occ, n_pan, gamma_ia, coef_virt, coef_occ, tile_mask, tile_owner):
    half = gamma_ia.shape[1]
    depth = gamma_ia.shape[2]
    panel_width = coef_virt.shape[0] // n_pan
    row_tiles = coef_occ.shape[0] // TILE
    col_tiles = panel_width // TILE
    parts = col_tiles // 2
    width = 2 * TILE
    pairs = n_pan // 2
    chunks = parts + pairs
    most = max(parts, pairs)
    group = n_pan // 2
    quarter = half // 2
    far = 2 * half
    bf16, f32 = jnp.bfloat16, jnp.float32
    dma = pltpu.SemaphoreType.DMA
    hbm = pl.BlockSpec(memory_space=pl.ANY)
    vmem = pl.BlockSpec(memory_space=pltpu.VMEM)
    pieces = len(pieces_of(depth))
    arrived = pl.pallas_call(
        functools.partial(kernel, n_occ, n_pan, parts),
        out_shape=pltpu.VMEM((n_pan, SCAP, AUX, TILE, TILE), bf16),
        in_specs=[vmem, vmem, hbm, hbm, hbm],
        out_specs=hbm,
        scratch_shapes=[
            pltpu.VMEM((n_occ, depth, half), bf16),
            pltpu.VMEM((n_occ * half, depth), bf16),
            pltpu.VMEM((depth, half), bf16),
            pltpu.VMEM((half, depth), bf16),
            pltpu.VMEM((n_pan, col_tiles, depth, TILE), bf16),
            pltpu.VMEM((row_tiles, TILE, coef_occ.shape[1]), bf16),
            pltpu.VMEM((row_tiles, TILE, depth), bf16),
            pltpu.VMEM((most, group, half, width), bf16),
            pltpu.VMEM((chunks, group, half, width), bf16),
            pltpu.VMEM((most, 2, quarter, width), f32),
            pltpu.VMEM((most, 2, quarter, width), f32),
            pltpu.VMEM((most, 2, quarter, width), bf16),
            pltpu.VMEM((chunks, 2, quarter, width), bf16),
            pltpu.VMEM((most, 2, quarter, width), bf16),
            pltpu.VMEM((chunks, 2, quarter, width), bf16),
            pltpu.VMEM((most, quarter, width), bf16),
            pltpu.VMEM((chunks, quarter, width), bf16),
            pltpu.VMEM((most, quarter, width), bf16),
            pltpu.VMEM((chunks, quarter, width), bf16),
            pltpu.VMEM((n_occ, col_tiles, half, TILE), bf16),
            pltpu.VMEM((n_pan, SCAP, TILE, TILE), bf16),
            pltpu.VMEM((n_pan, SCAP, TILE, TILE), bf16),
            pltpu.VMEM((row_tiles, TILE, far), bf16),
            pltpu.VMEM((n_pan, SCAP, TILE, TILE), bf16),
            pltpu.VMEM((n_pan, SCAP, TILE, TILE), bf16),
            pltpu.VMEM((n_pan, SCAP, TILE, TILE), f32),
            pltpu.VMEM((2 * n_pan, TILE), jnp.int32),
            pltpu.SMEM((2 * n_pan, TILE), jnp.int32),
            dma,
            dma((n_pan, col_tiles)), dma, dma, dma, dma, dma,
            *[dma((chunks,)) for _ in range(10)],
            dma((2, n_occ - 1, pieces)), dma((2, n_occ - 1, pieces)),
            dma((2, 2, parts)), dma((2, 2, parts)),
            dma((n_pan - 1,)), dma((n_pan - 1,)),
            dma((4,)), dma((4,)), dma((n_pan,)), dma((n_pan,)),
        ],
        compiler_params=pltpu.CompilerParams(
            collective_id=0, has_side_effects=True, vmem_limit_bytes=65000000
        ),
    )(
        tile_mask,
        tile_owner,
        jnp.swapaxes(gamma_ia, 1, 2),
        coef_virt.T,
        coef_occ.reshape(row_tiles, TILE, coef_occ.shape[1]),
    )
    return arrived[None, None]


def solution(mesh):
    n_occ, n_pan = mesh.shape["occ"], mesh.shape["pan"]

    def local(gamma_ia, coef_virt, coef_occ, tile_mask, tile_owner):
        fits = (
            n_occ == 4
            and n_pan == 8
            and gamma_ia.shape[1] == 2 * TILE
            and gamma_ia.shape[2] >= PIECE
            and coef_virt.shape[0] % (2 * TILE * n_pan) == 0
            and coef_occ.shape[0] % (4 * TILE) == 0
        )
        if fits:
            return by_kernel(n_occ, n_pan, gamma_ia, coef_virt, coef_occ, tile_mask, tile_owner)
        return by_collectives(gamma_ia, coef_virt, coef_occ, tile_mask, tile_owner)

    return jax.shard_map(
        local,
        mesh=mesh,
        in_specs=(P(None, "occ", "pan"), P(None, "pan"), P("occ", None), P(), P()),
        out_specs=P("occ", "pan", None, None, None, None, None),
        check_vma=False,
    )
```

```python
import functools

import jax
import jax.numpy as jnp
from jax import lax
from jax.experimental import pallas as pl
from jax.experimental.pallas import tpu as pltpu
from jax.sharding import PartitionSpec as P

AUX = 2
TILE = 128
SCAP = 2
PIECE = 256
LAGS = (1, 3, 5)
ROW_CODE = 64
KEPT_CODE = 4096
MESH = pl.DeviceIdType.MESH


def find_codes(blocks, mask, owner_in, row_tiles, col_tiles, owners):
    col = lax.broadcasted_iota(jnp.int32, mask.shape, 1)
    owner = jnp.where(mask == 1, owner_in, -1)
    codes = []
    for block in blocks:
        row = lax.broadcasted_iota(jnp.int32, mask.shape, 0) - block * row_tiles
        owner_of = jnp.where((row >= 0) & (row < row_tiles), owner, -1)
        place = row * ROW_CODE + col
        least, most = [], []
        for j in range(owners):
            chosen = owner_of == j
            least.append(jnp.min(jnp.where(chosen, place, 1 << 20), axis=0, keepdims=True))
            most.append(jnp.max(jnp.where(chosen, place, -1), axis=0, keepdims=True))
        least, most = jnp.concatenate(least), jnp.concatenate(most)
        lane = lax.broadcasted_iota(jnp.int32, least.shape, 1)
        slot = lax.broadcasted_iota(jnp.int32, (owners, TILE), 1)
        code = jnp.zeros((owners, TILE), jnp.int32)
        for s in range(owners):
            mine = (lane >= s * col_tiles) & (lane < (s + 1) * col_tiles)
            low = jnp.min(jnp.where(mine, least, 1 << 20), axis=1, keepdims=True)
            high = jnp.max(jnp.where(mine, most, -1), axis=1, keepdims=True)
            shift = KEPT_CODE - s * col_tiles
            code = jnp.where(slot == SCAP * s, jnp.where(high >= 0, low + shift, 0), code)
            code = jnp.where(slot == SCAP * s + 1, jnp.where(high > low, high + shift, 0), code)
        codes.append(code)
    return jnp.concatenate(codes)


def by_collectives(gamma_ia, coef_virt, coef_occ, tile_mask, tile_owner):
    panels = lax.axis_size("pan")
    occ_local = gamma_ia.shape[1]
    panel_width = coef_virt.shape[0] // panels
    row_tiles = coef_occ.shape[0] // TILE
    col_tiles = panel_width // TILE
    gamma_flat = gamma_ia.reshape(AUX * occ_local, gamma_ia.shape[2])
    summed = lax.psum_scatter(
        lax.dot_general(
            coef_virt, gamma_flat, (((1,), (1,)), ((), ())), preferred_element_type=jnp.float32
        ),
        "pan",
        scatter_dimension=0,
        tiled=True,
    )
    half_x = summed.astype(jnp.bfloat16).reshape(panel_width, AUX, occ_local)
    whole_x = lax.all_gather(half_x, "occ", axis=2, tiled=True)
    codes = find_codes(
        [lax.axis_index("occ")], tile_mask, tile_owner, row_tiles, col_tiles, panels
    )
    codes = lax.dynamic_slice(codes, (0, lax.axis_index("pan") * SCAP), (panels, SCAP)).reshape(-1)
    filled = codes // KEPT_CODE
    row = codes % KEPT_CODE // ROW_CODE
    col = codes % ROW_CODE
    bf16 = jnp.bfloat16
    row_pick = (row[:, None] == jnp.arange(row_tiles)[None, :]).astype(bf16)
    col_pick = (col[:, None] == jnp.arange(col_tiles)[None, :]).astype(bf16)
    row_set = jnp.einsum(
        "st,tri->sri", row_pick, coef_occ.reshape(row_tiles, TILE, coef_occ.shape[1])
    )
    col_set = jnp.einsum(
        "st,tkpi->skpi", col_pick, whole_x.reshape(col_tiles, TILE, AUX, whole_x.shape[2])
    )
    picked = jnp.einsum("sri,skpi->sprk", row_set, col_set, preferred_element_type=jnp.float32)
    picked = (
        picked.reshape(panels, SCAP, AUX, TILE, TILE)
        * filled.astype(jnp.float32).reshape(panels, SCAP)[:, :, None, None, None]
    )
    arrived = lax.all_to_all(
        picked.astype(jnp.bfloat16), "pan", split_axis=0, concat_axis=0, tiled=True
    )
    return arrived[None, None]


def pieces_of(depth):
    later = depth // PIECE - 1
    first = (depth - later * PIECE + TILE) // TILE * TILE
    starts = [0] + [first + n * PIECE for n in range(later)] + [depth]
    return [(a, b - a) for a, b in zip(starts[:-1], starts[1:])]


def kernel(
    n_occ, n_pan, parts,
    mask_ref, owner_ref, gamma_ref, virt_ref, occ_ref, out_ref,
    gam, flat, stage, gam_1, virt, coef, y_rows, send_c, recv_c, keep_a, keep_b,
    send_a, recv_a, send_b, recv_b, send_2a, recv_2a, send_2b, recv_2b,
    whole, picked, done, coef_far, send_f, recv_f, near_f, code_in, code_of, code_sem,
    load_sem, coef_sem, own_sem, done_sem, gam_sem, stage_sem,
    c_out, c_in, a_out, a_in, b_out, b_in, a2_out, a2_in, b2_out, b2_in,
    g_out, g_in, z_out, z_in, t_out, t_in, e_out, e_in, f_out, f_in,
):
    o = lax.axis_index("occ")
    s = lax.axis_index("pan")
    core = lax.rem(s, 2)
    x = lax.rem(s // 2, 2)
    y = s // 4
    other_core = s + 1 - 2 * core
    other_x = s + 2 - 4 * x
    other_y = s + 4 - 8 * y
    group = n_pan // 2
    half, depth = gam_1.shape
    quarter = half // 2
    tiles = half // TILE
    pairs = n_pan // 2
    last = n_occ - 1
    upper = o // 2
    middle = (o > 0) & (o < last)
    bf16, f32 = jnp.bfloat16, jnp.float32
    pieces = pieces_of(depth)

    def load(pan, t):
        first = pl.multiple_of((pan * (parts * tiles) + t) * TILE, TILE)
        return pltpu.make_async_copy(
            virt_ref.at[:, pl.ds(first, TILE)], virt.at[pan, t], load_sem.at[pan, t]
        )

    def load_part(q):
        for g in range(group):
            for t in range(tiles):
                load(2 * g + 1 - core, q * tiles + t).start()
        for g in range(group):
            for t in range(tiles):
                load(2 * g + core, q * tiles + t).start()

    take_0 = pltpu.make_async_copy(gamma_ref.at[0], gam.at[o], gam_sem)
    take_1 = pltpu.make_async_copy(gamma_ref.at[1], stage, stage_sem)
    fetch = pltpu.make_async_copy(occ_ref, coef, coef_sem)
    tell = pltpu.make_async_copy(code_in, code_of, code_sem)
    take_1.start()

    barrier = pltpu.get_barrier_semaphore()
    for d in range(1, n_pan):
        pl.semaphore_signal(
            barrier, inc=1, device_id=(o, lax.rem(s + d, n_pan)), device_id_type=MESH
        )
    for d in range(1, n_occ):
        pl.semaphore_signal(
            barrier, inc=1, device_id=(lax.rem(o + d, n_occ), s), device_id_type=MESH
        )
    load_part(0)
    take_0.start()
    pl.semaphore_wait(barrier, n_pan + n_occ - 2)

    def remote(src, dst, out_sem, in_sem, pan, row=None):
        return pltpu.make_async_remote_copy(
            src_ref=src, dst_ref=dst, send_sem=out_sem, recv_sem=in_sem,
            device_id=(o if row is None else row, pan), device_id_type=MESH,
        )

    def copy_c(n, base):
        ch = base + n
        return remote(send_c.at[n], recv_c.at[ch], c_out.at[ch], c_in.at[ch], other_core)

    def copy_a(n, base, h):
        ch = base + n
        return remote(
            send_a.at[n, h], recv_a.at[ch, h], a_out.at[ch, h], a_in.at[ch, h], other_x
        )

    def copy_b(n, base, h):
        ch = base + n
        return remote(
            send_b.at[n, h], recv_b.at[ch, h], b_out.at[ch, h], b_in.at[ch, h], other_y
        )

    def copy_2a(n, base):
        ch = base + n
        return remote(send_2a.at[n], recv_2a.at[ch], a2_out.at[ch], a2_in.at[ch], other_y)

    def copy_2b(n, base):
        ch = base + n
        return remote(send_2b.at[n], recv_2b.at[ch], b2_out.at[ch], b2_in.at[ch], other_x)

    def drain(base, count):
        def one(n, c):
            for copy in (copy_c, copy_2a, copy_2b):
                copy(n, base).wait_send()
            for h in range(2):
                copy_a(n, base, h).wait_send()
                copy_b(n, base, h).wait_send()
            return c

        lax.fori_loop(0, count, one, 0)

    def beyond(way):
        return jnp.clip(o + 1 - 2 * way, 0, last)

    def held(way, hop):
        return o - hop if way == 0 else o + hop

    def sends(way, hop):
        return (o < last) & (o >= hop) if way == 0 else (o > 0) & (o + hop <= last)

    def passes(way):
        return o == 1 if way == 0 else o == last - 1

    def ends_at(way):
        return o == last if way == 0 else o == 0

    def copy_g(n, way, hop):
        first, size = pieces[n]
        part = gam.at[held(way, hop), pl.ds(first, size)]
        mine = gamma_ref.at[0, pl.ds(first, size)]
        return remote(
            mine if hop == 0 else part, part,
            g_out.at[way, hop, n], g_in.at[way, hop, n], s, beyond(way),
        )

    def got_g(n, way, hop):
        first, size = pieces[n]
        part = gam.at[held(way, hop + 1), pl.ds(first, size)]
        return remote(
            part, part, g_out.at[way, hop, n], g_in.at[way, hop, n], s, beyond(way)
        )

    def pass_g(hop, when=True, some=range(len(pieces))):
        for way in range(2):
            @pl.when(sends(way, hop) & when)
            def _(way=way):
                for n in some:
                    if hop:
                        got_g(n, way, hop - 1).wait_recv()
                    copy_g(n, way, hop).start()

    def flip(z, n):
        first, size = pieces[n]
        rows = pl.ds(pl.multiple_of(z * half, half), half)
        flat[rows, first:first + size] = gam[z, first:first + size].T

    def copy_z(q, way, hop, source):
        part = whole.at[source, pl.ds(q * tiles, tiles)]
        return remote(
            part, part, z_out.at[way, hop, q], z_in.at[way, hop, q], s, beyond(way)
        )

    def each_part(todo):
        def one(q, c):
            todo(q)
            return c

        lax.fori_loop(0, parts, one, 0)

    parity = x + y - 2 * x * y
    some = coef.shape[0] // 4
    cols = 2 * half

    def band(odd):
        return pl.ds((2 * (parity + odd - 2 * parity * odd) + core) * some, some)

    def copy_e0(end):
        first = cols if end == 0 else 0
        return remote(
            occ_ref.at[band(0), :, pl.ds(first, cols)], coef_far.at[band(0)],
            e_out.at[0], e_in.at[0], s, 1 if end == 0 else last - 1,
        )

    def copy_e(step, odd, pan):
        return remote(
            coef_far.at[band(odd)], coef_far.at[band(odd)], e_out.at[step], e_in.at[step], pan
        )

    across = other_x + core * (other_y - other_x)

    pass_g(0)
    for end in (0, last):
        @pl.when(o == end)
        def _(end=end):
            copy_e0(end).start()

    take_1.wait()
    gam_1[...] = stage[...].T

    def second(n, base):
        ch = base + n
        copy_a(n, base, 1).wait_recv()
        send_2a[n] = (keep_a[n, 1] + recv_a[ch, 1].astype(f32)).astype(bf16)
        copy_2a(n, base).start()
        copy_b(n, base, 1).wait_recv()
        send_2b[n] = (keep_b[n, 1] + recv_b[ch, 1].astype(f32)).astype(bf16)
        copy_2b(n, base).start()
        copy_a(n, base, 0).wait_recv()
        keep_a[n, 0] = keep_a[n, 0] + recv_a[ch, 0].astype(f32)
        copy_b(n, base, 0).wait_recv()
        keep_b[n, 0] = keep_b[n, 0] + recv_b[ch, 0].astype(f32)

    def third(n, base, store):
        ch = base + n
        copy_2a(n, base).wait_recv()
        copy_2b(n, base).wait_recv()
        for h, keep, arrived in ((0, keep_a, recv_2a), (1, keep_b, recv_2b)):
            total = (keep[n, 0] + arrived[ch].astype(f32)).astype(bf16)
            for t in range(tiles):
                store(h, t, total[:, t * TILE:(t + 1) * TILE])

    def near(b, a):
        return (y + b - 2 * y * b) * 2 + x + a - 2 * x * a

    def product(q, pan):
        columns = jnp.concatenate([virt[pan, q * tiles + t] for t in range(tiles)], axis=1)
        return jnp.dot(gam_1[...], columns, preferred_element_type=f32)

    it_sent = max(parts - 2, 0)

    def half_step(it, carry):
        @pl.when(it + 1 < parts)
        def _():
            load_part(it + 1)

        @pl.when(it == parts)
        def _():
            fetch.start()

        @pl.when(it < parts)
        def _():
            for g in range(group):
                for t in range(tiles):
                    load(2 * g + 1 - core, it * tiles + t).wait()

            def one(g, c):
                send_c[it, g] = product(it, 2 * g + 1 - core).astype(bf16)
                return c

            for g in range(group):
                one(g, 0)
            copy_c(it, 0).start()

        @pl.when((it >= LAGS[0]) & (it < parts + LAGS[0]))
        def _():
            q = it - LAGS[0]
            for g in range(group):
                for t in range(tiles):
                    load(2 * g + core, q * tiles + t).wait()
            copy_c(q, 0).wait_recv()
            for b, a in ((1, 1), (0, 1), (1, 0), (0, 0)):
                g = near(b, a)
                total = product(q, 2 * g + core) + recv_c[q, g].astype(f32)
                if a:
                    send_a[q, b] = total[:quarter].astype(bf16)
                else:
                    keep_a[q, b] = total[:quarter]
                if b:
                    send_b[q, a] = total[quarter:].astype(bf16)
                else:
                    keep_b[q, a] = total[quarter:]
                if a:
                    copy_a(q, 0, b).start()
                if b:
                    copy_b(q, 0, a).start()

        pass_g(1, it == 3, (0, 1))
        pass_g(1, it == 5, range(2, len(pieces)))

        @pl.when((it >= LAGS[1]) & (it < parts + LAGS[1]))
        def _():
            second(it - LAGS[1], 0)

        @pl.when(it >= LAGS[2])
        def _():
            q = it - LAGS[2]

            def store(h, t, tile):
                whole[o, q * tiles + t, h * quarter:(h + 1) * quarter] = tile

            third(q, 0, store)
            for end, way in ((0, 0), (last, 1)):
                @pl.when(o == end)
                def _(way=way):
                    copy_z(q, way, 0, o).start()

        for way in range(2):
            @pl.when(passes(way) & (it == parts + 3))
            def _(way=way):
                for q in range(it_sent):
                    copy_z(q, way, 0, o).start()

        @pl.when(it == parts)
        def _():
            code_in[...] = find_codes(
                [o, upper * last], mask_ref[...], owner_ref[...],
                coef.shape[0], parts * tiles, n_pan,
            )
            tell.start()
            take_0.wait()
            for n in range(len(pieces)):
                flip(o, n)

        pass_g(2, it == parts + 2, (0, 1))
        pass_g(2, it == parts + 3, (2,))

        for side in (-1, 1):
            @pl.when(middle & (it == parts + 1))
            def _(side=side):
                for n in range(len(pieces)):
                    flip(o + side, n)

        return carry

    lax.fori_loop(0, parts + LAGS[2], half_step, 0)

    pass_g(2, True, range(3, len(pieces)))

    for way in range(2):
        @pl.when(passes(way))
        def _(way=way):
            for q in range(it_sent, parts):
                copy_z(q, way, 0, o).start()

    @pl.when(middle)
    def _():
        copy_e(0, 0, across).wait_recv()
        copy_e(1, 0, across).start()

    fetch.wait()
    tell.wait()
    for way in range(2):
        @pl.when(ends_at(way))
        def _(way=way):
            for hop in range(last - 1):
                for n in range(len(pieces)):
                    got_g(n, way, hop).wait_recv()
                    flip(held(way, hop + 1), n)

    far_plane = (1 - upper) * last
    count = len(pieces)
    per_step = 5 if coef.shape[0] // 2 % 5 == 0 else 2
    for span in (range(count - 2), range(count - 2, count - 1), range(count - 1, count)):
        for n in span:
            for way in range(2):
                @pl.when(ends_at(way))
                def _(way=way, n=n):
                    got_g(n, way, last - 1).wait_recv()

            flip(far_plane, n)

        def rows_step(r, carry, span=span):
            for n in range(per_step):
                pair = per_step * r + n
                left = jnp.concatenate([coef[2 * pair], coef[2 * pair + 1]])
                for m in span:
                    first, size = pieces[m]
                    made = jnp.dot(
                        left, flat[:, first:first + size], preferred_element_type=f32
                    ).astype(bf16)
                    y_rows[2 * pair, :, first:first + size] = made[:TILE]
                    y_rows[2 * pair + 1, :, first:first + size] = made[TILE:]
            return carry

        lax.fori_loop(0, coef.shape[0] // 2 // per_step, rows_step, 0)

    for way in range(2):
        @pl.when(passes(1 - way))
        def _(way=way):
            each_part(lambda q: copy_z(q, way, 0, o).start())

    for way in range(2):
        @pl.when(passes(way))
        def _(way=way):
            def on(q):
                copy_z(q, way, 0, held(way, 1)).wait_recv()
                copy_z(q, way, 1, held(way, 1)).start()

            each_part(on)

    @pl.when(middle)
    def _():
        copy_e(2, 0, other_core).start()
        copy_e(1, 1, across).wait_recv()
        copy_e(3, 1, other_core).start()

    drain(0, parts)

    def place(block, panel, j, k):
        code = code_of[block * n_pan + j, SCAP * panel + k]
        kept = lax.shift_right_logical(code, 12)
        row = lax.shift_right_logical(code - kept * KEPT_CODE, 6)
        return row, code - kept * KEPT_CODE - row * ROW_CODE, kept.astype(f32)

    def tile_part(panel, j, k):
        row, col, kept = place(0, panel, j, k)
        return jnp.dot(y_rows[row], virt[panel, col], preferred_element_type=f32) * kept

    def tile_rest(it, carry):
        @pl.when((it >= LAGS[1]) & (it < pairs + LAGS[1]))
        def _():
            second(it - LAGS[1], parts)

        @pl.when(it >= LAGS[2])
        def _():
            pair = it - LAGS[2]

            def store(h, t, tile):
                done[2 * pair + t, h] = tile

            third(pair, parts, store)

        return carry

    def tile_step(it, carry):
        @pl.when(it < pairs)
        def _():
            def one(g, c):
                for k in range(SCAP):
                    for t in range(2):
                        made = tile_part(2 * it + t, 2 * g + 1 - core, k)
                        send_c[
                            it, g, k * TILE:(k + 1) * TILE, t * TILE:(t + 1) * TILE
                        ] = made.astype(bf16)
                return c

            for g in range(group):
                one(g, 0)
            copy_c(it, parts).start()

        @pl.when((it >= LAGS[0]) & (it < pairs + LAGS[0]))
        def _():
            pair = it - LAGS[0]
            ch = parts + pair
            copy_c(pair, parts).wait_recv()
            for b, a in ((1, 1), (0, 1), (1, 0), (0, 0)):
                g = near(b, a)
                j = 2 * g + core
                for k in range(SCAP):
                    for t in range(2):
                        rows = slice(k * TILE, (k + 1) * TILE)
                        cols = slice(t * TILE, (t + 1) * TILE)
                        total = tile_part(2 * pair + t, j, k)
                        total = total + recv_c[ch, g, rows, cols].astype(f32)
                        if k == 0 and a:
                            send_a[pair, b, :, cols] = total.astype(bf16)
                        elif k == 0:
                            keep_a[pair, b, :, cols] = total
                        elif b:
                            send_b[pair, a, :, cols] = total.astype(bf16)
                        else:
                            keep_b[pair, a, :, cols] = total
                if a:
                    copy_a(pair, parts, b).start()
                if b:
                    copy_b(pair, parts, a).start()

        return tile_rest(it, carry)

    lax.fori_loop(0, pairs + LAGS[0], tile_step, 0)

    def copy_f(j):
        return remote(send_f.at[j], recv_f.at[j], f_out.at[j], f_in.at[j], s, upper * last)

    @pl.when(middle)
    def _():
        for way in range(2):
            @pl.when(passes(1 - way))
            def _(way=way):
                each_part(lambda q: copy_z(q, way, 0, held(way, 1)).wait_recv())
                each_part(lambda q: copy_z(q, way, 1, held(way, 2)).wait_recv())

        copy_e(2, 0, other_core).wait_recv()
        copy_e(3, 1, other_core).wait_recv()
        far = 2 - 2 * upper

        def far_owner(d, c):
            j = lax.rem(s + d, n_pan)
            for k in range(SCAP):
                row, col, kept = place(1, s, j, k)
                total = jnp.dot(
                    coef_far[row],
                    jnp.concatenate([whole[far + z, col] for z in range(2)]),
                    preferred_element_type=f32,
                )
                send_f[j, k] = (total * kept).astype(bf16)
            copy_f(j).start()
            return c

        lax.fori_loop(1, n_pan + 1, far_owner, 0)

    lax.fori_loop(pairs + LAGS[0], pairs + LAGS[1], tile_rest, 0)
    for way, end in ((1, 0), (0, last)):
        @pl.when(o == end)
        def _(way=way, end=end):
            each_part(lambda q: copy_z(q, way, 0, held(way, 1)).wait_recv())
            first = 0 if end == 0 else n_occ - 2

            def near_owner(j, c):
                for k in range(SCAP):
                    row, col, kept = place(0, s, j, k)
                    total = jnp.dot(
                        coef[row, :, first * half:(first + 2) * half],
                        jnp.concatenate([whole[first + z, col] for z in range(2)]),
                        preferred_element_type=f32,
                    )
                    near_f[j, k] = total * kept
                return c

            lax.fori_loop(0, n_pan, near_owner, 0)

    finished = pltpu.make_async_copy(done, out_ref.at[:, :, 0], done_sem)

    def tile_send(d, source, target):
        return remote(
            picked.at[target], out_ref.at[source, :, 1], t_out.at[d - 1], t_in.at[d - 1], target
        )

    own = pltpu.make_async_copy(picked.at[s], out_ref.at[s, :, 1], own_sem)

    def give(d, j):
        @pl.when(d < n_pan)
        def _():
            tile_send(d, s, j).start()

        @pl.when(d == n_pan)
        def _():
            own.start()

    @pl.when(middle)
    def _():
        def one_owner(d, c):
            j = lax.rem(s + d, n_pan)
            for k in range(SCAP):
                row, col, kept = place(0, s, j, k)
                total = jnp.dot(
                    coef[row],
                    jnp.concatenate([whole[z, col] for z in range(n_occ)]),
                    preferred_element_type=f32,
                )
                picked[j, k] = (total * kept).astype(bf16)
            give(d, j)
            return c

        lax.fori_loop(1, n_pan + 1, one_owner, 0)

    @pl.when(~middle)
    def _():
        def one_owner(d, c):
            j = lax.rem(s + d, n_pan)
            copy_f(j).wait_recv()
            for k in range(SCAP):
                picked[j, k] = (near_f[j, k] + recv_f[j, k].astype(f32)).astype(bf16)
            give(d, j)
            return c

        lax.fori_loop(1, n_pan - 2, one_owner, 0)
        lax.fori_loop(pairs + LAGS[1], pairs + LAGS[2], tile_rest, 0)
        finished.start()
        lax.fori_loop(n_pan - 2, n_pan + 1, one_owner, 0)

    for end in (0, last):
        @pl.when(o == end)
        def _(end=end):
            copy_e0(end).wait_send()

    @pl.when(middle)
    def _():
        lax.fori_loop(pairs + LAGS[1], pairs + LAGS[2], tile_rest, 0)
        finished.start()
        copy_e(1, 0, across).wait_send()
        copy_e(2, 0, other_core).wait_send()
        copy_e(3, 1, other_core).wait_send()

        def sent(j, c):
            copy_f(j).wait_send()
            return c

        lax.fori_loop(0, n_pan, sent, 0)

    drain(parts, pairs)

    for way in range(2):
        for hop in range(last):
            @pl.when(sends(way, hop))
            def _(hop=hop, way=way):
                for n in range(len(pieces)):
                    copy_g(n, way, hop).wait_send()

        @pl.when(sends(way, 0))
        def _(way=way):
            each_part(lambda q: copy_z(q, way, 0, o).wait_send())

        @pl.when(passes(way))
        def _(way=way):
            each_part(lambda q: copy_z(q, way, 1, held(way, 1)).wait_send())

    def finish(d, c):
        tile_send(d, s, lax.rem(s + d, n_pan)).wait_send()
        source = lax.rem(s + n_pan - d, n_pan)
        tile_send(d, source, source).wait_recv()
        return c

    lax.fori_loop(1, n_pan, finish, 0)
    finished.wait()
    own.wait()


def by_kernel(n_occ, n_pan, gamma_ia, coef_virt, coef_occ, tile_mask, tile_owner):
    half = gamma_ia.shape[1]
    depth = gamma_ia.shape[2]
    panel_width = coef_virt.shape[0] // n_pan
    row_tiles = coef_occ.shape[0] // TILE
    col_tiles = panel_width // TILE
    parts = col_tiles // 2
    width = 2 * TILE
    pairs = n_pan // 2
    chunks = parts + pairs
    most = max(parts, pairs)
    group = n_pan // 2
    quarter = half // 2
    far = 2 * half
    bf16, f32 = jnp.bfloat16, jnp.float32
    dma = pltpu.SemaphoreType.DMA
    hbm = pl.BlockSpec(memory_space=pl.ANY)
    vmem = pl.BlockSpec(memory_space=pltpu.VMEM)
    pieces = len(pieces_of(depth))
    arrived = pl.pallas_call(
        functools.partial(kernel, n_occ, n_pan, parts),
        out_shape=pltpu.VMEM((n_pan, SCAP, AUX, TILE, TILE), bf16),
        in_specs=[vmem, vmem, hbm, hbm, hbm],
        out_specs=hbm,
        scratch_shapes=[
            pltpu.VMEM((n_occ, depth, half), bf16),
            pltpu.VMEM((n_occ * half, depth), bf16),
            pltpu.VMEM((depth, half), bf16),
            pltpu.VMEM((half, depth), bf16),
            pltpu.VMEM((n_pan, col_tiles, depth, TILE), bf16),
            pltpu.VMEM((row_tiles, TILE, coef_occ.shape[1]), bf16),
            pltpu.VMEM((row_tiles, TILE, depth), bf16),
            pltpu.VMEM((most, group, half, width), bf16),
            pltpu.VMEM((chunks, group, half, width), bf16),
            pltpu.VMEM((most, 2, quarter, width), f32),
            pltpu.VMEM((most, 2, quarter, width), f32),
            pltpu.VMEM((most, 2, quarter, width), bf16),
            pltpu.VMEM((chunks, 2, quarter, width), bf16),
            pltpu.VMEM((most, 2, quarter, width), bf16),
            pltpu.VMEM((chunks, 2, quarter, width), bf16),
            pltpu.VMEM((most, quarter, width), bf16),
            pltpu.VMEM((chunks, quarter, width), bf16),
            pltpu.VMEM((most, quarter, width), bf16),
            pltpu.VMEM((chunks, quarter, width), bf16),
            pltpu.VMEM((n_occ, col_tiles, half, TILE), bf16),
            pltpu.VMEM((n_pan, SCAP, TILE, TILE), bf16),
            pltpu.VMEM((n_pan, SCAP, TILE, TILE), bf16),
            pltpu.VMEM((row_tiles, TILE, far), bf16),
            pltpu.VMEM((n_pan, SCAP, TILE, TILE), bf16),
            pltpu.VMEM((n_pan, SCAP, TILE, TILE), bf16),
            pltpu.VMEM((n_pan, SCAP, TILE, TILE), f32),
            pltpu.VMEM((2 * n_pan, TILE), jnp.int32),
            pltpu.SMEM((2 * n_pan, TILE), jnp.int32),
            dma,
            dma((n_pan, col_tiles)), dma, dma, dma, dma, dma,
            *[dma((chunks,)) for _ in range(2)],
            *[dma((chunks, 2)) for _ in range(4)],
            *[dma((chunks,)) for _ in range(4)],
            dma((2, n_occ - 1, pieces)), dma((2, n_occ - 1, pieces)),
            dma((2, 2, parts)), dma((2, 2, parts)),
            dma((n_pan - 1,)), dma((n_pan - 1,)),
            dma((4,)), dma((4,)), dma((n_pan,)), dma((n_pan,)),
        ],
        compiler_params=pltpu.CompilerParams(
            collective_id=0, has_side_effects=True, vmem_limit_bytes=65000000
        ),
    )(
        tile_mask,
        tile_owner,
        jnp.swapaxes(gamma_ia, 1, 2),
        coef_virt.T,
        coef_occ.reshape(row_tiles, TILE, coef_occ.shape[1]),
    )
    return arrived[None, None]


def solution(mesh):
    n_occ, n_pan = mesh.shape["occ"], mesh.shape["pan"]

    def local(gamma_ia, coef_virt, coef_occ, tile_mask, tile_owner):
        fits = (
            n_occ == 4
            and n_pan == 8
            and gamma_ia.shape[1] == 2 * TILE
            and gamma_ia.shape[2] >= PIECE
            and coef_virt.shape[0] % (2 * TILE * n_pan) == 0
            and coef_occ.shape[0] % (4 * TILE) == 0
        )
        if fits:
            return by_kernel(n_occ, n_pan, gamma_ia, coef_virt, coef_occ, tile_mask, tile_owner)
        return by_collectives(gamma_ia, coef_virt, coef_occ, tile_mask, tile_owner)

    return jax.shard_map(
        local,
        mesh=mesh,
        in_specs=(P(None, "occ", "pan"), P(None, "pan"), P("occ", None), P(), P()),
        out_specs=P("occ", "pan", None, None, None, None, None),
        check_vma=False,
    )
```
